32 devices in a mesh: groups: 2 (over y), space: 4 (over z), shot: 4 (over x, core).
Axes of the slice: x: 2, y: 2, z: 4, core: 2. Of those that a mesh axis runs over, the one named last changes fastest.
Arguments:
- wavefields: float32 [8, 2, 2, 64, 16, 256], P(('groups', 'shot'), None, None, 'space'), parts along dimension 0, may hold values from -6 to 6
- velocity: float32 [128, 16, 256], P(('groups', 'space'), 'shot'), parts along dimension 0, may hold values from 0.05 to 0.18
- aperture: int32 [8, 2], P(('groups', 'shot')), parts along dimension 0, may hold values from 0 to 64, as said below
Outputs:
- final_fields: float32 [8, 2, 2, 64, 16, 256], P(('groups', 'shot'), None, None, 'space'), parts along dimension 0
- image: float32 [128, 16, 256], P(('groups', 'space'), 'shot'), parts along dimension 0
The draws below stay inside these ranges and needn't reach their ends.
There are 2 independent parts, one for each index of `groups`. The reference program is written for one: setup_inputs(seed, part) draws one part's arguments, and reference() takes and returns one part's arrays. A program takes and returns all parts, laid end to end along the dimension named above; each array names one. Nothing has to cross between parts.
Inputs may be any that keep to these rules, and one draw needn't show every extreme that they name: Row s holds shot s's aperture [lo, hi): lo below 16 and hi above 48.
All inputs are finite; a program needn't handle non-finite values.
Results may differ from the reference program's by a relative error of at most 0.0003.
Values sent between devices are 32-bit elements; how exact they have to be, the bound alone decides.
A program may use at most 64 MiB of HBM per device.

```python
import jax
import jax.numpy as jnp
from jax import lax

Y = 16
Z = 256
STEPS = 8
SHOTS = 4
X = 64


def draw_aperture(key, part):
    first_key, second_key = jax.random.split(jax.random.fold_in(key, 7))
    lower = jax.random.randint(first_key, (SHOTS,), 0, X // 4)
    upper = X - jax.random.randint(second_key, (SHOTS,), 0, X // 4)
    return jnp.stack([lower, upper], axis=1).astype(jnp.int32)


def level_of(stream_key, dims, cuts, smallest, high):
    factor_of = 1.0
    for axis_at, shards_of in cuts:
        steps = jax.random.uniform(jax.random.fold_in(jax.random.fold_in(stream_key, 6), axis_at), (shards_of,), jnp.float32, smallest / len(cuts), high / len(cuts))
        factor_of = factor_of * jnp.repeat(jnp.exp(steps), dims[axis_at] // shards_of).reshape((-1,) + (1,) * (len(dims) - 1 - axis_at))
    return factor_of


def scatter_about(own_key, dims, spread, most, cuts=(), held_as=jnp.bfloat16):
    drawn = jax.random.normal(own_key, dims, jnp.float32) * spread
    if len(cuts) > 0:
        drawn = level_of(own_key, dims, cuts, -0.22, 0.18) * drawn
    return jnp.clip(drawn, min=-most, max=most).astype(held_as)


def setup_inputs(seed: int = 0, part: int = 0) -> dict:
    key_list = jax.random.split(jax.random.key(seed), 4)
    part_splits = jax.random.split(jax.random.fold_in(key_list[3], part), 4)
    wavefields = scatter_about(part_splits[0], (SHOTS, 2, 2, X, Y, Z), 1.0, 6.0, ((0, 4), (3, 4)), jnp.float32)
    velocity = jnp.clip(0.05 + 0.13000001 * jax.random.uniform(part_splits[1], (X, Y, Z), jnp.float32) ** level_of(part_splits[1], (X, Y, Z), ((0, 4), (1, 4)), -0.2, 0.2), 0.05, 0.18)
    aperture = draw_aperture(jax.random.fold_in(jax.random.fold_in(key_list[3], part), 71), part)
    return {"wavefields": wavefields, "velocity": velocity, "aperture": aperture}


coefficients = (-205.0 / 72.0, 8.0 / 5.0, -1.0 / 5.0, 8.0 / 315.0, -1.0 / 560.0)


def laplace(padded):
    rows_x = padded.shape[1] - 8
    rows_y = padded.shape[2]
    rows_z = padded.shape[3]
    padded_all = jnp.pad(padded, ((0, 0), (0, 0), (4, 4), (4, 4)))
    center = padded_all[:, 4:4 + rows_x, 4:4 + rows_y, 4:4 + rows_z]
    summed = (3.0 * coefficients[0]) * center
    for reach in range(1, 5):
        beside_all = padded_all[:, 4 + reach:4 + reach + rows_x, 4:4 + rows_y, 4:4 + rows_z]
        beside_all = beside_all + padded_all[:, 4 - reach:4 - reach + rows_x, 4:4 + rows_y, 4:4 + rows_z]
        beside_all = beside_all + padded_all[:, 4:4 + rows_x, 4 + reach:4 + reach + rows_y, 4:4 + rows_z]
        beside_all = beside_all + padded_all[:, 4:4 + rows_x, 4 - reach:4 - reach + rows_y, 4:4 + rows_z]
        beside_all = beside_all + padded_all[:, 4:4 + rows_x, 4:4 + rows_y, 4 + reach:4 + reach + rows_z]
        beside_all = beside_all + padded_all[:, 4:4 + rows_x, 4:4 + rows_y, 4 - reach:4 - reach + rows_z]
        summed = summed + coefficients[reach] * beside_all
    return summed


def reference(wavefields, velocity, aperture):
    def one_shot(packed):
        fields, bounds = packed
        previous = fields[0]
        current = fields[1]
        global_x = jnp.arange(X, dtype=jnp.int32)
        inside = ((global_x >= bounds[0]) & (global_x < bounds[1])).astype(jnp.float32)[:, None, None]
        partial_value = jnp.zeros((X, Y, Z), jnp.float32)
        for step_index in range(STEPS):
            padded = jnp.pad(current, ((0, 0), (4, 4), (0, 0), (0, 0)))
            following = inside * (2.0 * current - previous + velocity * laplace(padded))
            partial_value = partial_value + following[0] * following[1]
            previous = current
            current = following
        return jnp.stack([previous, current]), partial_value

    finals, partials = lax.map(one_shot, (wavefields, aperture))
    return finals, jnp.sum(partials, axis=0) / STEPS
```

```python
import functools

import jax
import jax.numpy as jnp
import numpy as np
from jax import lax
from jax.experimental import pallas as pl
from jax.experimental.pallas import tpu as pltpu
from jax.sharding import PartitionSpec as P

STEPS = 8
REACH = 4


SCALE = 5040.0
CENTRE = -3.0 * 14350.0
WEIGHTS = (0.0, 8064.0, -1008.0, 128.0, -9.0)
MESH = pl.DeviceIdType.MESH


def band(size):
    matrix = np.zeros((size, size), np.float32)
    for reach in range(1, REACH + 1):
        matrix += np.float32(WEIGHTS[reach]) * (
            np.eye(size, k=reach, dtype=np.float32) + np.eye(size, k=-reach, dtype=np.float32)
        )
    return matrix


def kernel(
    left, right, waves, velocity, aperture, out, image,
    left_ref, right_ref, halo, speeds, speed, gain, inside, lap, total,
    middle, middle_arrived, edges, edges_arrived,
    halo_send, halo_recv, speed_send, speed_recv, part_send, part_recv, local_sem,
):
    space = lax.axis_index("space")
    spaces = lax.axis_size("space")
    shot = lax.axis_index("shot")
    shots = lax.axis_size("shot")
    cells_x, rows_y, rows_z = out.shape[2:]
    slab = velocity.shape[1]
    flat = (cells_x * rows_y, rows_z)
    chunks = halo_send.shape[3]
    tall = rows_y // chunks
    inner = slice(REACH, cells_x - REACH)
    border = (slice(0, REACH), slice(cells_x - REACH, cells_x))
    has = (space > 0, space < spaces - 1)
    beside = (space - 1, space + 1)

    loads = [
        pltpu.make_async_copy(source, target, local_sem.at[at])
        for at, (source, target) in enumerate(
            ((waves, out), (velocity, speeds.at[shot]), (left, left_ref), (right, right_ref))
        )
    ]
    for load in loads:
        load.start()

    barrier = pltpu.get_barrier_semaphore()
    for side in range(2):
        @pl.when(has[side])
        def _():
            pl.semaphore_signal(barrier, inc=1, device_id={"space": beside[side]}, device_id_type=MESH)

    for ahead in range(1, shots):
        peer = lax.rem(shot + ahead, shots)
        pl.semaphore_signal(barrier, inc=1, device_id={"shot": peer}, device_id_type=MESH)
    pl.semaphore_wait(barrier, shots - 1 + jnp.where(has[0], 1, 0) + jnp.where(has[1], 1, 0))

    def rows_of(chunk):
        return pl.ds(chunk * tall, tall)

    def halo_copy(source, slot, field, side, chunk):
        return pltpu.make_async_remote_copy(
            source.at[field, border[side], rows_of(chunk)],
            halo.at[slot, field, 1 - side, :, rows_of(chunk)],
            halo_send.at[slot, field, side, chunk],
            halo_recv.at[slot, field, 1 - side, chunk],
            device_id={"space": beside[side]},
            device_id_type=MESH,
        )

    def sent(source, slot, field):
        for side in range(2):
            @pl.when(has[side])
            def _():
                for chunk in range(chunks):
                    halo_copy(source, slot, field, side, chunk).wait_send()

    for field in range(2):
        for chunk in range(chunks):
            for side in range(2):
                @pl.when(has[side])
                def _():
                    halo_copy(waves.at[1], 0, field, side, chunk).start()

    spans = border + (inner,)
    speed_copies = []
    for kind, span in enumerate(spans):
        for ahead in range(1, shots):
            copy = pltpu.make_async_remote_copy(
                velocity.at[span],
                speeds.at[shot, span],
                speed_send.at[kind, ahead - 1],
                speed_recv.at[kind, ahead - 1],
                device_id={"shot": lax.rem(shot + ahead, shots)},
                device_id_type=MESH,
            )
            copy.start()
            speed_copies.append(copy)

    def gather(kind):
        span = spans[kind]
        for copy in speed_copies[kind * (shots - 1) : (kind + 1) * (shots - 1)]:
            copy.wait()
        for index in range(shots):
            speed[span, index * slab : (index + 1) * slab, :] = speeds[index, span]
        scaled = speed[span] * inside[span] * (1.0 / SCALE)
        speed[span] = scaled
        gain[span] = 2.0 * inside[span] + CENTRE * scaled

    total[...] = jnp.zeros(total.shape, jnp.float32)
    global_x = space * cells_x + lax.broadcasted_iota(jnp.int32, inside.shape, 0)
    within = (global_x >= aperture[0, 0]) & (global_x < aperture[0, 1])
    inside[...] = jnp.where(within, 1.0, 0.0)

    def spread(now, field):
        cells = out[now, field].reshape(flat)
        high = cells.astype(jnp.bfloat16)
        low = (cells - high.astype(jnp.float32)).astype(jnp.bfloat16)
        return (
            jnp.dot(left_ref[...], jnp.concatenate([high, low], axis=0), preferred_element_type=jnp.float32)
            + jnp.dot(jnp.concatenate([high, low], axis=1), right_ref[...], preferred_element_type=jnp.float32)
        ).reshape(lap.shape[1:])

    def base(now, then, field, cells, around, masked):
        before = out[then, field, cells]
        if masked:
            before = inside[cells] * before
        out[then, field, cells] = gain[cells] * out[now, field, cells] - before + speed[cells] * around

    def correlate(then, cells):
        total[cells] = total[cells] + out[then, 0, cells] * out[then, 1, cells]

    def advance(now, then, field, masked=False):
        base(now, then, field, slice(0, cells_x), spread(now, field), masked)
        if field == 1:
            correlate(then, inner)

    def finish(index, then, field, side, chunk):
        halo_copy(out.at[then], index, field, 1 - side, chunk).wait_recv()
        rows = rows_of(chunk)
        layers = [halo[index, field, side, layer, rows] for layer in range(REACH)]
        for cell in range(REACH):
            at = cell + side * (cells_x - REACH)
            if side == 0:
                terms = [WEIGHTS[cell + REACH - layer] * layers[layer] for layer in range(cell, REACH)]
            else:
                terms = [WEIGHTS[REACH + layer - cell] * layers[layer] for layer in range(cell + 1)]
            out[then, field, at, rows] = out[then, field, at, rows] + speed[at, rows] * sum(terms[1:], terms[0])

    def borders(index, then, field, send=True):
        for chunk in range(chunks):
            for side in range(2):
                @pl.when(has[side])
                def _():
                    finish(index, then, field, side, chunk)
                    if send:
                        halo_copy(out.at[then], index + 1, field, side, chunk).start()

    def step(index, carry):
        then = lax.rem(index, 2)
        now = 1 - then
        for field in range(2):
            borders(index, then, field)
            sent(out.at[now], index, field)
            if field == 1:
                for side in range(2):
                    correlate(then, border[side])
            advance(then, now, field)
        return carry

    loads[0].wait()
    loads[2].wait()
    loads[3].wait()
    for field in range(2):
        lap[field] = spread(1, field)
    loads[1].wait()
    for kind in range(2):
        gather(kind)
        for field in range(2):
            base(1, 0, field, border[kind], lap[field, border[kind]], True)
    for field in range(2):
        borders(0, 0, field)
    gather(2)
    for field in range(2):
        base(1, 0, field, inner, lap[field, inner], True)
    for side in range(2):
        correlate(0, border[side])
    correlate(0, inner)
    for field in range(2):
        sent(waves.at[1], 0, field)
        advance(0, 1, field, True)

    lax.fori_loop(1, STEPS - 1, step, 0)

    last = STEPS - 1
    then = last % 2

    def part_copy(kind, source, target, ahead):
        peer = lax.rem(shot + ahead, shots)
        return pltpu.make_async_remote_copy(
            source.at[peer],
            target.at[ahead - 1],
            part_send.at[kind, ahead - 1],
            part_recv.at[kind, ahead - 1],
            device_id={"shot": peer},
            device_id_type=MESH,
        )

    for index in range(shots):
        middle[index] = total[inner, index * slab : (index + 1) * slab, :]
    copies = [part_copy(0, middle, middle_arrived, ahead) for ahead in range(1, shots)]
    for copy in copies:
        copy.start()
    for field in range(2):
        borders(last, then, field, False)
    for side in range(2):
        correlate(then, border[side])
    for index in range(shots):
        rows = slice(index * slab, (index + 1) * slab)
        for side in range(2):
            edges[index, side * REACH : (side + 1) * REACH] = total[border[side], rows, :]
    edge_copies = [part_copy(1, edges, edges_arrived, ahead) for ahead in range(1, shots)]
    for copy in edge_copies:
        copy.start()
    for field in range(2):
        sent(out.at[1 - then], last, field)
    summed = middle[shot]
    for copy, ahead in zip(copies, range(1, shots)):
        copy.wait()
        summed = summed + middle_arrived[ahead - 1]
    image[inner] = summed / STEPS
    summed = edges[shot]
    for copy, ahead in zip(edge_copies, range(1, shots)):
        copy.wait()
        summed = summed + edges_arrived[ahead - 1]
    for side in range(2):
        image[border[side]] = summed[side * REACH : (side + 1) * REACH] / STEPS


def keep(fields, image, fields_out, image_out, store_sem):
    stores = [pltpu.make_async_copy(image, image_out, store_sem.at[0])] + [
        pltpu.make_async_copy(fields.at[time], fields_out.at[time], store_sem.at[1 + time]) for time in range(2)
    ]
    for store in stores:
        store.start()
    for store in stores:
        store.wait()


def shards(wavefields, velocity, aperture):
    fields = wavefields[0]
    cells_x, rows_y, rows_z = fields.shape[2:]
    shots = lax.axis_size("shot")
    slab = velocity.shape[1]
    chunks = max(rows_y // 8, 1)
    across = np.kron(band(cells_x), np.eye(rows_y, dtype=np.float32)) + np.kron(
        np.eye(cells_x, dtype=np.float32), band(rows_y)
    )
    left = np.concatenate([across, across], axis=1).astype(jnp.bfloat16)
    right = np.concatenate([band(rows_z)] * 2, axis=0).astype(jnp.bfloat16)
    grid = (cells_x, rows_y, rows_z)
    vmem = pl.BlockSpec(memory_space=pltpu.VMEM)
    anywhere = pl.BlockSpec(memory_space=pl.ANY)
    finals, image = pl.pallas_call(
        kernel,
        out_shape=(pltpu.VMEM(fields.shape, jnp.float32), pltpu.VMEM(velocity.shape, jnp.float32)),
        in_specs=[anywhere, anywhere, anywhere, anywhere, pl.BlockSpec(memory_space=pltpu.SMEM)],
        out_specs=(vmem, vmem),
        scratch_shapes=[
            pltpu.VMEM(left.shape, jnp.bfloat16),
            pltpu.VMEM(right.shape, jnp.bfloat16),
            pltpu.VMEM((STEPS, 2, 2, REACH, rows_y, rows_z), jnp.float32),
            pltpu.VMEM((shots,) + velocity.shape, jnp.float32),
            pltpu.VMEM(grid, jnp.float32),
            pltpu.VMEM(grid, jnp.float32),
            pltpu.VMEM(grid, jnp.float32),
            pltpu.VMEM((2,) + grid, jnp.float32),
            pltpu.VMEM(grid, jnp.float32),
            pltpu.VMEM((shots, cells_x - 2 * REACH, slab, rows_z), jnp.float32),
            pltpu.VMEM((shots - 1, cells_x - 2 * REACH, slab, rows_z), jnp.float32),
            pltpu.VMEM((shots, 2 * REACH, slab, rows_z), jnp.float32),
            pltpu.VMEM((shots - 1, 2 * REACH, slab, rows_z), jnp.float32),
            pltpu.SemaphoreType.DMA((STEPS, 2, 2, chunks)),
            pltpu.SemaphoreType.DMA((STEPS, 2, 2, chunks)),
            pltpu.SemaphoreType.DMA((3, shots - 1)),
            pltpu.SemaphoreType.DMA((3, shots - 1)),
            pltpu.SemaphoreType.DMA((2, shots - 1)),
            pltpu.SemaphoreType.DMA((2, shots - 1)),
            pltpu.SemaphoreType.DMA((4,)),
        ],
        compiler_params=pltpu.CompilerParams(collective_id=0, has_side_effects=True),
    )(jnp.asarray(left), jnp.asarray(right), fields, velocity, aperture)
    finals, image = pl.pallas_call(
        keep,
        out_shape=(
            jax.ShapeDtypeStruct(fields.shape, jnp.float32),
            jax.ShapeDtypeStruct(velocity.shape, jnp.float32),
        ),
        in_specs=[vmem, vmem],
        out_specs=(anywhere, anywhere),
        scratch_shapes=[pltpu.SemaphoreType.DMA((3,))],
    )(
        pltpu.with_memory_space_constraint(finals, pltpu.VMEM),
        pltpu.with_memory_space_constraint(image, pltpu.VMEM),
    )
    return finals[None], image


def solution(mesh):
    in_specs = (
        P(("groups", "shot"), None, None, "space", None, None),
        P(("groups", "space"), "shot", None),
        P(("groups", "shot"), None),
    )
    out_specs = (
        P(("groups", "shot"), None, None, "space", None, None),
        P(("groups", "space"), "shot", None),
    )
    return jax.shard_map(shards, mesh=mesh, in_specs=in_specs, out_specs=out_specs, check_vma=False)
```

```python
import functools

import jax
import jax.numpy as jnp
import numpy as np
from jax import lax
from jax.experimental import pallas as pl
from jax.experimental.pallas import tpu as pltpu
from jax.sharding import PartitionSpec as P

STEPS = 8
REACH = 4


SCALE = 5040.0
CENTRE = -3.0 * 14350.0
WEIGHTS = (0.0, 8064.0, -1008.0, 128.0, -9.0)
MESH = pl.DeviceIdType.MESH


def band(size):
    matrix = np.zeros((size, size), np.float32)
    for reach in range(1, REACH + 1):
        matrix += np.float32(WEIGHTS[reach]) * (
            np.eye(size, k=reach, dtype=np.float32) + np.eye(size, k=-reach, dtype=np.float32)
        )
    return matrix


def kernel(
    left, right, waves, velocity, aperture, ext, image,
    left_ref, right_ref, outer, speeds, speed, gain, inside, lap, total,
    middle, middle_arrived, edges, edges_arrived,
    halo_send, halo_recv, speed_send, speed_recv, part_send, part_recv, local_sem,
):
    space = lax.axis_index("space")
    spaces = lax.axis_size("space")
    shot = lax.axis_index("shot")
    shots = lax.axis_size("shot")
    wide, rows_y, rows_z = ext.shape[2:]
    cells_x, slab = velocity.shape[:2]
    flat = (wide * rows_y, rows_z)
    own = slice(REACH, REACH + cells_x)
    ghost = (slice(0, REACH), slice(wide - REACH, wide))
    border = (slice(REACH, 2 * REACH), slice(wide - 2 * REACH, wide - REACH))
    beyond = (slice(2 * REACH, 3 * REACH), slice(wide - 3 * REACH, wide - 2 * REACH))
    inner = slice(2 * REACH, wide - 2 * REACH)
    last = STEPS - 1
    chunks = halo_send.shape[0] - STEPS + 1
    tall = rows_y // chunks
    owners = shots // chunks
    has = (space > 0, space < spaces - 1)
    beside = (space - 1, space + 1)

    def within(span):
        return slice(span.start - REACH, span.stop - REACH)

    loads = [
        pltpu.make_async_copy(source, target, local_sem.at[at])
        for at, (source, target) in enumerate(
            (
                (waves.at[1], ext.at[1, :, own]),
                (left, left_ref),
                (right, right_ref),
                (waves.at[0], ext.at[0, :, own]),
                (velocity, speeds.at[shot, own]),
            )
        )
    ]
    for load in loads:
        load.start()

    barrier = pltpu.get_barrier_semaphore()
    for side in range(2):
        @pl.when(has[side])
        def _():
            pl.semaphore_signal(barrier, inc=1, device_id={"space": beside[side]}, device_id_type=MESH)

    for ahead in range(1, shots):
        peer = lax.rem(shot + ahead, shots)
        pl.semaphore_signal(barrier, inc=1, device_id={"shot": peer}, device_id_type=MESH)
    pl.semaphore_wait(barrier, shots - 1 + jnp.where(has[0], 1, 0) + jnp.where(has[1], 1, 0))

    def message(source, target, slot, field, side):
        return pltpu.make_async_remote_copy(
            source,
            target,
            halo_send.at[slot, field, side],
            halo_recv.at[slot, field, 1 - side],
            device_id={"space": beside[side]},
            device_id_type=MESH,
        )

    def first_copy(field, side):
        return message(waves.at[1, field, within(border[side])], outer.at[STEPS - 2, field, 1 - side], 0, field, side)

    def second_copy(field, side):
        return message(ext.at[0, field, border[side]], ext.at[0, field, ghost[1 - side]], 1, field, side)

    def outer_copy(index, field, side):
        return message(
            ext.at[lax.rem(index + 1, 2), field, beyond[side]],
            outer.at[index - 1, field, 1 - side],
            index + 1,
            field,
            side,
        )

    def rows_of(turn):
        chunk = lax.rem(shot * slab // tall + 1 + turn, chunks)
        return pl.ds(pl.multiple_of(chunk * tall, tall), tall)

    def last_copy(turn, field, side):
        rows = rows_of(turn)
        return message(
            ext.at[last % 2, field, beyond[side], rows],
            outer.at[last - 2, field, 1 - side, :, rows],
            STEPS - 1 + turn,
            field,
            side,
        )

    def on_sides(act):
        for side in range(2):
            @pl.when(has[side])
            def _():
                act(side)

    def speed_copy(kind, side_or_span, ahead):
        return pltpu.make_async_remote_copy(
            velocity.at[within(side_or_span)],
            speeds.at[shot, side_or_span],
            speed_send.at[kind, ahead - 1],
            speed_recv.at[kind, ahead - 1],
            device_id={"shot": lax.rem(shot + ahead, shots)},
            device_id_type=MESH,
        )

    def next_speed(side):
        return pltpu.make_async_remote_copy(
            velocity.at[within(border[side])],
            speeds.at[shot, ghost[1 - side]],
            speed_send.at[5, side],
            speed_recv.at[5, 1 - side],
            device_id={"space": beside[side]},
            device_id_type=MESH,
        )

    def ghost_speed(side, ahead):
        return pltpu.make_async_remote_copy(
            speeds.at[shot, ghost[side]],
            speeds.at[shot, ghost[side]],
            speed_send.at[3 + side, ahead - 1],
            speed_recv.at[3 + side, ahead - 1],
            device_id={"shot": lax.rem(shot + ahead, shots)},
            device_id_type=MESH,
        )

    spans = border + (inner,)
    on_sides(lambda side: first_copy(0, side).start())
    for kind in range(2):
        for ahead in range(1, shots):
            speed_copy(kind, spans[kind], ahead).start()
    on_sides(lambda side: first_copy(1, side).start())
    on_sides(lambda side: next_speed(side).start())
    for ahead in range(1, shots):
        speed_copy(2, spans[2], ahead).start()

    global_x = space * cells_x - REACH + lax.broadcasted_iota(jnp.int32, inside.shape, 0)
    seen = (global_x >= aperture[0, 0]) & (global_x < aperture[0, 1])
    inside[...] = jnp.where(seen, 1.0, 0.0)

    none = jnp.zeros((REACH, rows_y, rows_z), jnp.float32)
    for side in range(2):
        for field in range(2):
            ext[1, field, ghost[side]] = none

        @pl.when(jnp.logical_not(has[side]))
        def _():
            speed[ghost[side]] = none
            gain[ghost[side]] = none
            for field in range(2):
                ext[0, field, ghost[side]] = none

    def weigh(span):
        for index in range(shots):
            speed[span, index * slab : (index + 1) * slab, :] = speeds[index, span]
        scaled = speed[span] * inside[span] * (1.0 / SCALE)
        speed[span] = scaled
        gain[span] = 2.0 * inside[span] + CENTRE * scaled

    def gather(kind):
        for ahead in range(1, shots):
            speed_copy(kind, spans[kind], ahead).wait()
        weigh(spans[kind])

    def gather_ghost(side):
        for ahead in range(1, shots):
            ghost_speed(side, ahead).wait()
        weigh(ghost[side])

    def spread(now, field):
        cells = ext[now, field].reshape(flat)
        high = cells.astype(jnp.bfloat16)
        low = (cells - high.astype(jnp.float32)).astype(jnp.bfloat16)
        return (
            jnp.dot(left_ref[...], jnp.concatenate([high, low], axis=0), preferred_element_type=jnp.float32)
            + jnp.dot(jnp.concatenate([high, low], axis=1), right_ref[...], preferred_element_type=jnp.float32)
        ).reshape(ext.shape[2:])

    def base(now, then, field, cells, around, masked=False):
        before = ext[then, field, cells]
        if masked:
            before = inside[cells] * before
        ext[then, field, cells] = gain[cells] * ext[now, field, cells] - before + speed[cells] * around

    def correlate(then, cells):
        at = within(cells)
        total[at] = total[at] + ext[then, 0, cells] * ext[then, 1, cells]

    def terms(side, cell, layers):
        if side == 0:
            parts = [WEIGHTS[cell + REACH - layer] * layers[layer] for layer in range(cell, REACH)]
        else:
            parts = [WEIGHTS[REACH + layer - cell] * layers[layer] for layer in range(cell + 1)]
        return sum(parts[1:], parts[0])

    def added(slot, field, side, target, rows):
        layers = [outer[slot, field, side, layer, rows] for layer in range(REACH)]
        return [speed[target.start + cell, rows] * terms(side, cell, layers) for cell in range(REACH)]

    def put(then, field, target, rows, more):
        for cell in range(REACH):
            at = target.start + cell
            ext[then, field, at, rows] = ext[then, field, at, rows] + more[cell]

    every = slice(0, rows_y)

    def arrive(index, then, field):
        def act(side):
            outer_copy(index, field, 1 - side).wait_recv()
            put(then, field, ghost[side], every, added(index - 1, field, side, ghost[side], every))
        on_sides(act)

    for at in range(3):
        loads[at].wait()

    def hand_on(side):
        next_speed(1 - side).wait_recv()
        for ahead in range(1, shots):
            ghost_speed(side, ahead).start()

    for field in range(2):
        lap[field] = spread(1, field)
    loads[3].wait()
    loads[4].wait()
    for kind in range(2):
        gather(kind)
        for field in range(2):
            base(1, 0, field, border[kind], lap[field, border[kind]], True)

    def second(field):
        def act(side):
            first_copy(field, 1 - side).wait_recv()
            put(0, field, border[side], every, added(STEPS - 2, field, side, border[side], every))
            second_copy(field, side).start()
        on_sides(act)

    for field in range(2):
        second(field)
    on_sides(hand_on)
    gather(2)
    for field in range(2):
        base(1, 0, field, inner, lap[field, inner], True)
        on_sides(lambda side: outer_copy(1, field, side).start())

    def settle(side):
        for field in range(2):
            ext[1, field, ghost[side]] = outer[STEPS - 2, field, side]

    on_sides(settle)
    total[...] = ext[0, 0, own] * ext[0, 1, own]
    on_sides(gather_ghost)

    everything = slice(0, wide)
    for field in range(2):
        on_sides(lambda side: second_copy(field, 1 - side).wait_recv())
        base(0, 1, field, everything, spread(0, field), True)
        on_sides(lambda side: outer_copy(2, field, side).start())
    correlate(1, own)
    for field in range(2):
        on_sides(lambda side: second_copy(field, side).wait_send())

    def step(index, carry):
        then = lax.rem(index, 2)
        now = 1 - then
        for field in range(2):
            arrive(index - 1, now, field)
            on_sides(lambda side: outer_copy(index - 1, field, side).wait_send())
            base(now, then, field, everything, spread(now, field))

            @pl.when(index < last - 2)
            def _():
                on_sides(lambda side: outer_copy(index + 1, field, side).start())

            @pl.when(index == last - 2)
            def _():
                if field == 0:
                    on_sides(lambda side: last_copy(0, 0, side).start())
                else:
                    on_sides(lambda side: last_copy(0, 1, side).start())
                    for turn in range(1, chunks):
                        for late in range(2):
                            on_sides(lambda side: last_copy(turn, late, side).start())

        correlate(then, own)
        return carry

    lax.fori_loop(2, STEPS - 1, step, 0)

    then = last % 2
    now = 1 - then

    def part_copy(kind, source, target, ahead):
        peer = lax.rem(shot + ahead, shots)
        return pltpu.make_async_remote_copy(
            source.at[peer],
            target.at[ahead - 1],
            part_send.at[kind, ahead - 1],
            part_recv.at[kind, ahead - 1],
            device_id={"shot": peer},
            device_id_type=MESH,
        )

    for field in range(2):
        for turn in range(chunks):
            on_sides(lambda side: last_copy(turn, field, side).wait_send())
        base(now, then, field, own, spread(now, field)[own])
    correlate(then, inner)
    for index in range(shots):
        middle[index] = total[within(inner), index * slab : (index + 1) * slab, :]
    copies = [part_copy(0, middle, middle_arrived, ahead) for ahead in range(1, shots)]
    for copy in copies:
        copy.start()

    def complete(turn, field):
        rows = rows_of(turn)

        def act(side):
            last_copy(turn, field, 1 - side).wait_recv()
            layers = added(last - 2, field, side, ghost[side], rows)
            more = [speed[border[side].start + cell, rows] * terms(side, cell, layers) for cell in range(REACH)]
            put(then, field, border[side], rows, more)

        on_sides(act)

    for turn in range(chunks):
        for field in range(2):
            complete(turn, field)
        rows = rows_of(turn)
        chunk = lax.rem(shot * slab // tall + 1 + turn, chunks)
        for side in range(2):
            span = border[side]
            value = total[within(span), rows] + ext[then, 0, span, rows] * ext[then, 1, span, rows]
            for index in range(owners):
                edges[chunk * owners + index, side * REACH : (side + 1) * REACH] = value[
                    :, index * slab : (index + 1) * slab
                ]
        for index in range(owners):
            peer = chunk * owners + index

            @pl.when(peer != shot)
            def _():
                part_copy(1, edges, edges_arrived, lax.rem(peer - shot + shots, shots)).start()

    edge_copies = [part_copy(1, edges, edges_arrived, ahead) for ahead in range(1, shots)]

    def close(side):
        next_speed(side).wait_send()
        for field in range(2):
            first_copy(field, side).wait_send()

    on_sides(close)
    summed = middle[shot]
    for copy, ahead in zip(copies, range(1, shots)):
        copy.wait()
        summed = summed + middle_arrived[ahead - 1]
    image[within(inner)] = summed / STEPS
    summed = edges[shot]
    for copy, ahead in zip(edge_copies, range(1, shots)):
        copy.wait()
        summed = summed + edges_arrived[ahead - 1]
    for side in range(2):
        image[within(border[side])] = summed[side * REACH : (side + 1) * REACH] / STEPS


def keep(ext, image, fields_out, image_out, store_sem):
    cells_x = fields_out.shape[2]
    stores = [pltpu.make_async_copy(image, image_out, store_sem.at[0])] + [
        pltpu.make_async_copy(ext.at[time, :, REACH : REACH + cells_x], fields_out.at[time], store_sem.at[1 + time])
        for time in range(2)
    ]
    for store in stores:
        store.start()
    for store in stores:
        store.wait()


def shards(wavefields, velocity, aperture):
    fields = wavefields[0]
    cells_x, rows_y, rows_z = fields.shape[2:]
    wide = cells_x + 2 * REACH
    shots = lax.axis_size("shot")
    slab = velocity.shape[1]
    chunks = max(rows_y // max(8, slab), 1)
    across = np.kron(band(wide), np.eye(rows_y, dtype=np.float32)) + np.kron(
        np.eye(wide, dtype=np.float32), band(rows_y)
    )
    left = np.concatenate([across, across], axis=1).astype(jnp.bfloat16)
    right = np.concatenate([band(rows_z)] * 2, axis=0).astype(jnp.bfloat16)
    grid = (wide, rows_y, rows_z)
    vmem = pl.BlockSpec(memory_space=pltpu.VMEM)
    anywhere = pl.BlockSpec(memory_space=pl.ANY)
    ext, image = pl.pallas_call(
        kernel,
        out_shape=(pltpu.VMEM((2, 2) + grid, jnp.float32), pltpu.VMEM(velocity.shape, jnp.float32)),
        in_specs=[anywhere, anywhere, anywhere, anywhere, pl.BlockSpec(memory_space=pltpu.SMEM)],
        out_specs=(vmem, vmem),
        scratch_shapes=[
            pltpu.VMEM(left.shape, jnp.bfloat16),
            pltpu.VMEM(right.shape, jnp.bfloat16),
            pltpu.VMEM((STEPS - 1, 2, 2, REACH, rows_y, rows_z), jnp.float32),
            pltpu.VMEM((shots, wide, slab, rows_z), jnp.float32),
            pltpu.VMEM(grid, jnp.float32),
            pltpu.VMEM(grid, jnp.float32),
            pltpu.VMEM(grid, jnp.float32),
            pltpu.VMEM((2,) + grid, jnp.float32),
            pltpu.VMEM((cells_x, rows_y, rows_z), jnp.float32),
            pltpu.VMEM((shots, cells_x - 2 * REACH, slab, rows_z), jnp.float32),
            pltpu.VMEM((shots - 1, cells_x - 2 * REACH, slab, rows_z), jnp.float32),
            pltpu.VMEM((shots, 2 * REACH, slab, rows_z), jnp.float32),
            pltpu.VMEM((shots - 1, 2 * REACH, slab, rows_z), jnp.float32),
            pltpu.SemaphoreType.DMA((STEPS - 1 + chunks, 2, 2)),
            pltpu.SemaphoreType.DMA((STEPS - 1 + chunks, 2, 2)),
            pltpu.SemaphoreType.DMA((6, max(shots - 1, 2))),
            pltpu.SemaphoreType.DMA((6, max(shots - 1, 2))),
            pltpu.SemaphoreType.DMA((2, shots - 1)),
            pltpu.SemaphoreType.DMA((2, shots - 1)),
            pltpu.SemaphoreType.DMA((5,)),
        ],
        compiler_params=pltpu.CompilerParams(collective_id=0, has_side_effects=True),
    )(jnp.asarray(left), jnp.asarray(right), fields, velocity, aperture)
    finals, image = pl.pallas_call(
        keep,
        out_shape=(
            jax.ShapeDtypeStruct(fields.shape, jnp.float32),
            jax.ShapeDtypeStruct(velocity.shape, jnp.float32),
        ),
        in_specs=[vmem, vmem],
        out_specs=(anywhere, anywhere),
        scratch_shapes=[pltpu.SemaphoreType.DMA((3,))],
    )(
        pltpu.with_memory_space_constraint(ext, pltpu.VMEM),
        pltpu.with_memory_space_constraint(image, pltpu.VMEM),
    )
    return finals[None], image


def solution(mesh):
    in_specs = (
        P(("groups", "shot"), None, None, "space", None, None),
        P(("groups", "space"), "shot", None),
        P(("groups", "shot"), None),
    )
    out_specs = (
        P(("groups", "shot"), None, None, "space", None, None),
        P(("groups", "space"), "shot", None),
    )
    return jax.shard_map(shards, mesh=mesh, in_specs=in_specs, out_specs=out_specs, check_vma=False)
```

```python
import functools

import jax
import jax.numpy as jnp
import numpy as np
from jax import lax
from jax.experimental import pallas as pl
from jax.experimental.pallas import tpu as pltpu
from jax.sharding import PartitionSpec as P

STEPS = 8
REACH = 4


SCALE = 5040.0
CENTRE = -3.0 * 14350.0
WEIGHTS = (0.0, 8064.0, -1008.0, 128.0, -9.0)
MESH = pl.DeviceIdType.MESH


def band(size):
    matrix = np.zeros((size, size), np.float32)
    for reach in range(1, REACH + 1):
        matrix += np.float32(WEIGHTS[reach]) * (
            np.eye(size, k=reach, dtype=np.float32) + np.eye(size, k=-reach, dtype=np.float32)
        )
    return matrix


def kernel(
    left, right, waves, velocity, aperture, ext, image,
    left_ref, right_ref, outer, speeds, speed, gain, inside, lap, total,
    middle, middle_arrived, edges, edges_arrived,
    halo_send, halo_recv, speed_send, speed_recv, part_send, part_recv, local_sem,
):
    space = lax.axis_index("space")
    spaces = lax.axis_size("space")
    shot = lax.axis_index("shot")
    shots = lax.axis_size("shot")
    wide, rows_y, rows_z = ext.shape[2:]
    cells_x, slab = velocity.shape[:2]
    flat = (wide * rows_y, rows_z)
    own = slice(REACH, REACH + cells_x)
    ghost = (slice(0, REACH), slice(wide - REACH, wide))
    border = (slice(REACH, 2 * REACH), slice(wide - 2 * REACH, wide - REACH))
    beyond = (slice(2 * REACH, 3 * REACH), slice(wide - 3 * REACH, wide - 2 * REACH))
    inner = slice(2 * REACH, wide - 2 * REACH)
    last = STEPS - 1
    chunks = halo_send.shape[0] - STEPS + 1
    tall = rows_y // chunks
    owners = shots // chunks
    has = (space > 0, space < spaces - 1)
    beside = (space - 1, space + 1)

    def within(span):
        return slice(span.start - REACH, span.stop - REACH)

    loads = [
        pltpu.make_async_copy(source, target, local_sem.at[at])
        for at, (source, target) in enumerate(
            (
                (waves.at[1], ext.at[0, :, own]),
                (left, left_ref),
                (right, right_ref),
                (waves.at[0], ext.at[2, :, own]),
                (velocity, speeds.at[shot, own]),
            )
        )
    ]
    for load in loads:
        load.start()

    barrier = pltpu.get_barrier_semaphore()
    for side in range(2):
        @pl.when(has[side])
        def _():
            pl.semaphore_signal(barrier, inc=1, device_id={"space": beside[side]}, device_id_type=MESH)

    for ahead in range(1, shots):
        peer = lax.rem(shot + ahead, shots)
        pl.semaphore_signal(barrier, inc=1, device_id={"shot": peer}, device_id_type=MESH)
    pl.semaphore_wait(barrier, shots - 1 + jnp.where(has[0], 1, 0) + jnp.where(has[1], 1, 0))

    def message(source, target, slot, field, side):
        return pltpu.make_async_remote_copy(
            source,
            target,
            halo_send.at[slot, field, side],
            halo_recv.at[slot, field, 1 - side],
            device_id={"space": beside[side]},
            device_id_type=MESH,
        )

    def first_copy(field, side):
        return message(waves.at[1, field, within(border[side])], outer.at[STEPS - 2, field, 1 - side], 0, field, side)

    def second_copy(field, side):
        return message(ext.at[1, field, border[side]], ext.at[1, field, ghost[1 - side]], 1, field, side)

    def outer_copy(index, field, side):
        return message(
            ext.at[lax.rem(index, 3), field, beyond[side]],
            outer.at[index - 1, field, 1 - side],
            index + 1,
            field,
            side,
        )

    def rows_of(turn):
        chunk = lax.rem(shot * slab // tall + 1 + turn, chunks)
        return pl.ds(pl.multiple_of(chunk * tall, tall), tall)

    def last_copy(turn, field, side):
        rows = rows_of(turn)
        return message(
            ext.at[(last - 1) % 3, field, beyond[side], rows],
            outer.at[last - 2, field, 1 - side, :, rows],
            STEPS - 1 + turn,
            field,
            side,
        )

    def on_sides(act):
        for side in range(2):
            @pl.when(has[side])
            def _():
                act(side)

    def speed_copy(kind, side_or_span, ahead):
        return pltpu.make_async_remote_copy(
            velocity.at[within(side_or_span)],
            speeds.at[shot, side_or_span],
            speed_send.at[kind, ahead - 1],
            speed_recv.at[kind, ahead - 1],
            device_id={"shot": lax.rem(shot + ahead, shots)},
            device_id_type=MESH,
        )

    def next_speed(side):
        return pltpu.make_async_remote_copy(
            velocity.at[within(border[side])],
            speeds.at[shot, ghost[1 - side]],
            speed_send.at[5, side],
            speed_recv.at[5, 1 - side],
            device_id={"space": beside[side]},
            device_id_type=MESH,
        )

    def ghost_speed(side, ahead):
        return pltpu.make_async_remote_copy(
            speeds.at[shot, ghost[side]],
            speeds.at[shot, ghost[side]],
            speed_send.at[3 + side, ahead - 1],
            speed_recv.at[3 + side, ahead - 1],
            device_id={"shot": lax.rem(shot + ahead, shots)},
            device_id_type=MESH,
        )

    spans = border + (inner,)
    on_sides(lambda side: first_copy(0, side).start())
    for kind in range(2):
        for ahead in range(1, shots):
            speed_copy(kind, spans[kind], ahead).start()
    on_sides(lambda side: first_copy(1, side).start())
    on_sides(lambda side: next_speed(side).start())
    for ahead in range(1, shots):
        speed_copy(2, spans[2], ahead).start()

    global_x = space * cells_x - REACH + lax.broadcasted_iota(jnp.int32, inside.shape, 0)
    seen = (global_x >= aperture[0, 0]) & (global_x < aperture[0, 1])
    inside[...] = jnp.where(seen, 1.0, 0.0)

    none = jnp.zeros((REACH, rows_y, rows_z), jnp.float32)
    for side in range(2):
        for field in range(2):
            ext[0, field, ghost[side]] = none

        @pl.when(jnp.logical_not(has[side]))
        def _():
            speed[ghost[side]] = none
            gain[ghost[side]] = none
            for field in range(2):
                ext[1, field, ghost[side]] = none

    def weigh(span):
        for index in range(shots):
            speed[span, index * slab : (index + 1) * slab, :] = speeds[index, span]
        scaled = speed[span] * inside[span] * (1.0 / SCALE)
        speed[span] = scaled
        gain[span] = 2.0 * inside[span] + CENTRE * scaled

    def gather(kind):
        for ahead in range(1, shots):
            speed_copy(kind, spans[kind], ahead).wait()
        weigh(spans[kind])

    def gather_ghost(side):
        for ahead in range(1, shots):
            ghost_speed(side, ahead).wait()
        weigh(ghost[side])

    def spread(now, field):
        cells = ext[now, field].reshape(flat)
        high = cells.astype(jnp.bfloat16)
        low = (cells - high.astype(jnp.float32)).astype(jnp.bfloat16)
        return (
            jnp.dot(left_ref[...], jnp.concatenate([high, low], axis=0), preferred_element_type=jnp.float32)
            + jnp.dot(jnp.concatenate([high, low], axis=1), right_ref[...], preferred_element_type=jnp.float32)
        ).reshape(ext.shape[2:])

    def base(index, field, cells, around, masked=False):
        now, then, earlier = (lax.rem(index + ahead, 3) for ahead in range(3))
        before = ext[earlier, field, cells]
        if masked:
            before = inside[cells] * before
        ext[then, field, cells] = gain[cells] * ext[now, field, cells] - before + speed[cells] * around

    def correlate(then, cells):
        at = within(cells)
        total[at] = total[at] + ext[then, 0, cells] * ext[then, 1, cells]

    def terms(side, cell, layers):
        if side == 0:
            parts = [WEIGHTS[cell + REACH - layer] * layers[layer] for layer in range(cell, REACH)]
        else:
            parts = [WEIGHTS[REACH + layer - cell] * layers[layer] for layer in range(cell + 1)]
        return sum(parts[1:], parts[0])

    def added(slot, field, side, target, rows):
        layers = [outer[slot, field, side, layer, rows] for layer in range(REACH)]
        return [speed[target.start + cell, rows] * terms(side, cell, layers) for cell in range(REACH)]

    def put(then, field, target, rows, more):
        for cell in range(REACH):
            at = target.start + cell
            ext[then, field, at, rows] = ext[then, field, at, rows] + more[cell]

    every = slice(0, rows_y)

    def arrive(index, then, field):
        def act(side):
            outer_copy(index, field, 1 - side).wait_recv()
            put(then, field, ghost[side], every, added(index - 1, field, side, ghost[side], every))
        on_sides(act)

    for at in range(3):
        loads[at].wait()

    def hand_on(side):
        next_speed(1 - side).wait_recv()
        for ahead in range(1, shots):
            ghost_speed(side, ahead).start()

    for field in range(2):
        lap[field] = spread(0, field)
    loads[3].wait()
    loads[4].wait()
    for kind in range(2):
        gather(kind)
        for field in range(2):
            base(0, field, border[kind], lap[field, border[kind]], True)

    def second(field):
        def act(side):
            first_copy(field, 1 - side).wait_recv()
            put(1, field, border[side], every, added(STEPS - 2, field, side, border[side], every))
            second_copy(field, side).start()
        on_sides(act)

    for field in range(2):
        second(field)
    on_sides(hand_on)
    gather(2)
    for field in range(2):
        base(0, field, inner, lap[field, inner], True)
        on_sides(lambda side: outer_copy(1, field, side).start())

    def settle(side):
        for field in range(2):
            ext[0, field, ghost[side]] = outer[STEPS - 2, field, side]

    on_sides(settle)
    total[...] = ext[1, 0, own] * ext[1, 1, own]
    on_sides(gather_ghost)

    everything = slice(0, wide)
    for field in range(2):
        on_sides(lambda side: second_copy(field, 1 - side).wait_recv())
        base(1, field, everything, spread(1, field), True)
        on_sides(lambda side: outer_copy(2, field, side).start())
    correlate(2, own)
    for field in range(2):
        on_sides(lambda side: second_copy(field, side).wait_send())

    def step(index, carry):
        now = lax.rem(index, 3)
        for field in range(2):
            arrive(index - 1, now, field)

            @pl.when(index > 2)
            def _():
                on_sides(lambda side: outer_copy(index - 2, field, side).wait_send())

            base(index, field, everything, spread(now, field))

            @pl.when(index < last - 2)
            def _():
                on_sides(lambda side: outer_copy(index + 1, field, side).start())

            @pl.when(index == last - 2)
            def _():
                if field == 0:
                    on_sides(lambda side: last_copy(0, 0, side).start())
                else:
                    on_sides(lambda side: last_copy(0, 1, side).start())
                    for turn in range(1, chunks):
                        for late in range(2):
                            on_sides(lambda side: last_copy(turn, late, side).start())

        correlate(lax.rem(index + 1, 3), own)
        return carry

    lax.fori_loop(2, last - 1, step, 0)

    then = STEPS % 3

    def part_copy(kind, source, target, ahead):
        peer = lax.rem(shot + ahead, shots)
        return pltpu.make_async_remote_copy(
            source.at[peer],
            target.at[ahead - 1],
            part_send.at[kind, ahead - 1],
            part_recv.at[kind, ahead - 1],
            device_id={"shot": peer},
            device_id_type=MESH,
        )

    for field in range(2):
        arrive(last - 2, (last - 1) % 3, field)
        for index in (last - 1, last):
            on_sides(lambda side: outer_copy(index - 2, field, side).wait_send())
            cells = everything if index < last else own
            base(index, field, cells, spread(index % 3, field)[cells])
    correlate(last % 3, own)
    correlate(then, inner)
    for index in range(shots):
        middle[index] = total[within(inner), index * slab : (index + 1) * slab, :]
    copies = [part_copy(0, middle, middle_arrived, ahead) for ahead in range(1, shots)]
    for copy in copies:
        copy.start()

    def complete(turn, field):
        rows = rows_of(turn)

        def act(side):
            last_copy(turn, field, 1 - side).wait_recv()
            layers = added(last - 2, field, side, ghost[side], rows)
            more = [speed[border[side].start + cell, rows] * terms(side, cell, layers) for cell in range(REACH)]
            put(then, field, border[side], rows, more)

        on_sides(act)

    for turn in range(chunks):
        for field in range(2):
            complete(turn, field)
        rows = rows_of(turn)
        chunk = lax.rem(shot * slab // tall + 1 + turn, chunks)
        for side in range(2):
            span = border[side]
            value = total[within(span), rows] + ext[then, 0, span, rows] * ext[then, 1, span, rows]
            for index in range(owners):
                edges[chunk * owners + index, side * REACH : (side + 1) * REACH] = value[
                    :, index * slab : (index + 1) * slab
                ]
        for index in range(owners):
            peer = chunk * owners + index

            @pl.when(peer != shot)
            def _():
                part_copy(1, edges, edges_arrived, lax.rem(peer - shot + shots, shots)).start()

    edge_copies = [part_copy(1, edges, edges_arrived, ahead) for ahead in range(1, shots)]

    def close(side):
        next_speed(side).wait_send()
        for field in range(2):
            first_copy(field, side).wait_send()
            for turn in range(chunks):
                last_copy(turn, field, side).wait_send()

    on_sides(close)
    summed = middle[shot]
    for copy, ahead in zip(copies, range(1, shots)):
        copy.wait()
        summed = summed + middle_arrived[ahead - 1]
    image[within(inner)] = summed / STEPS
    summed = edges[shot]
    for copy, ahead in zip(edge_copies, range(1, shots)):
        copy.wait()
        summed = summed + edges_arrived[ahead - 1]
    for side in range(2):
        image[within(border[side])] = summed[side * REACH : (side + 1) * REACH] / STEPS


def keep(ext, image, fields_out, image_out, store_sem):
    cells_x = fields_out.shape[2]
    stores = [pltpu.make_async_copy(image, image_out, store_sem.at[0])] + [
        pltpu.make_async_copy(ext.at[(STEPS - 1 + time) % 3, :, REACH : REACH + cells_x], fields_out.at[time], store_sem.at[1 + time])
        for time in range(2)
    ]
    for store in stores:
        store.start()
    for store in stores:
        store.wait()


def shards(wavefields, velocity, aperture):
    fields = wavefields[0]
    cells_x, rows_y, rows_z = fields.shape[2:]
    wide = cells_x + 2 * REACH
    shots = lax.axis_size("shot")
    slab = velocity.shape[1]
    chunks = max(rows_y // max(8, slab), 1)
    across = np.kron(band(wide), np.eye(rows_y, dtype=np.float32)) + np.kron(
        np.eye(wide, dtype=np.float32), band(rows_y)
    )
    left = np.concatenate([across, across], axis=1).astype(jnp.bfloat16)
    right = np.concatenate([band(rows_z)] * 2, axis=0).astype(jnp.bfloat16)
    grid = (wide, rows_y, rows_z)
    vmem = pl.BlockSpec(memory_space=pltpu.VMEM)
    anywhere = pl.BlockSpec(memory_space=pl.ANY)
    ext, image = pl.pallas_call(
        kernel,
        out_shape=(pltpu.VMEM((3, 2) + grid, jnp.float32), pltpu.VMEM(velocity.shape, jnp.float32)),
        in_specs=[anywhere, anywhere, anywhere, anywhere, pl.BlockSpec(memory_space=pltpu.SMEM)],
        out_specs=(vmem, vmem),
        scratch_shapes=[
            pltpu.VMEM(left.shape, jnp.bfloat16),
            pltpu.VMEM(right.shape, jnp.bfloat16),
            pltpu.VMEM((STEPS - 1, 2, 2, REACH, rows_y, rows_z), jnp.float32),
            pltpu.VMEM((shots, wide, slab, rows_z), jnp.float32),
            pltpu.VMEM(grid, jnp.float32),
            pltpu.VMEM(grid, jnp.float32),
            pltpu.VMEM(grid, jnp.float32),
            pltpu.VMEM((2,) + grid, jnp.float32),
            pltpu.VMEM((cells_x, rows_y, rows_z), jnp.float32),
            pltpu.VMEM((shots, cells_x - 2 * REACH, slab, rows_z), jnp.float32),
            pltpu.VMEM((shots - 1, cells_x - 2 * REACH, slab, rows_z), jnp.float32),
            pltpu.VMEM((shots, 2 * REACH, slab, rows_z), jnp.float32),
            pltpu.VMEM((shots - 1, 2 * REACH, slab, rows_z), jnp.float32),
            pltpu.SemaphoreType.DMA((STEPS - 1 + chunks, 2, 2)),
            pltpu.SemaphoreType.DMA((STEPS - 1 + chunks, 2, 2)),
            pltpu.SemaphoreType.DMA((6, max(shots - 1, 2))),
            pltpu.SemaphoreType.DMA((6, max(shots - 1, 2))),
            pltpu.SemaphoreType.DMA((2, shots - 1)),
            pltpu.SemaphoreType.DMA((2, shots - 1)),
            pltpu.SemaphoreType.DMA((5,)),
        ],
        compiler_params=pltpu.CompilerParams(collective_id=0, has_side_effects=True),
    )(jnp.asarray(left), jnp.asarray(right), fields, velocity, aperture)
    finals, image = pl.pallas_call(
        keep,
        out_shape=(
            jax.ShapeDtypeStruct(fields.shape, jnp.float32),
            jax.ShapeDtypeStruct(velocity.shape, jnp.float32),
        ),
        in_specs=[vmem, vmem],
        out_specs=(anywhere, anywhere),
        scratch_shapes=[pltpu.SemaphoreType.DMA((3,))],
    )(
        pltpu.with_memory_space_constraint(ext, pltpu.VMEM),
        pltpu.with_memory_space_constraint(image, pltpu.VMEM),
    )
    return finals[None], image


def solution(mesh):
    in_specs = (
        P(("groups", "shot"), None, None, "space", None, None),
        P(("groups", "space"), "shot", None),
        P(("groups", "shot"), None),
    )
    out_specs = (
        P(("groups", "shot"), None, None, "space", None, None),
        P(("groups", "space"), "shot", None),
    )
    return jax.shard_map(shards, mesh=mesh, in_specs=in_specs, out_specs=out_specs, check_vma=False)
```

```python
import functools

import jax
import jax.numpy as jnp
import numpy as np
from jax import lax
from jax.experimental import pallas as pl
from jax.experimental.pallas import tpu as pltpu
from jax.sharding import PartitionSpec as P

STEPS = 8
REACH = 4


SCALE = 5040.0
CENTRE = -3.0 * 14350.0
WEIGHTS = (0.0, 8064.0, -1008.0, 128.0, -9.0)
MESH = pl.DeviceIdType.MESH


def band(size):
    matrix = np.zeros((size, size), np.float32)
    for reach in range(1, REACH + 1):
        matrix += np.float32(WEIGHTS[reach]) * (
            np.eye(size, k=reach, dtype=np.float32) + np.eye(size, k=-reach, dtype=np.float32)
        )
    return matrix


def kernel(
    left, right, waves, velocity, aperture, ext, image,
    left_ref, right_ref, outer, speeds, speed, gain, inside, lap, total,
    middle, middle_arrived, edges, edges_arrived,
    halo_send, halo_recv, speed_send, speed_recv, part_send, part_recv, local_sem,
):
    space = lax.axis_index("space")
    spaces = lax.axis_size("space")
    shot = lax.axis_index("shot")
    shots = lax.axis_size("shot")
    wide, rows_y, rows_z = ext.shape[2:]
    cells_x, slab = velocity.shape[:2]
    flat = (wide * rows_y, rows_z)
    own = slice(REACH, REACH + cells_x)
    ghost = (slice(0, REACH), slice(wide - REACH, wide))
    border = (slice(REACH, 2 * REACH), slice(wide - 2 * REACH, wide - REACH))
    beyond = (slice(2 * REACH, 3 * REACH), slice(wide - 3 * REACH, wide - 2 * REACH))
    inner = slice(2 * REACH, wide - 2 * REACH)
    last = STEPS - 1
    chunks = halo_send.shape[0] - STEPS + 1
    tall = rows_y // chunks
    owners = shots // chunks
    has = (space > 0, space < spaces - 1)
    beside = (space - 1, space + 1)

    def within(span):
        return slice(span.start - REACH, span.stop - REACH)

    loads = [
        pltpu.make_async_copy(source, target, local_sem.at[at])
        for at, (source, target) in enumerate(
            (
                (waves.at[1], ext.at[0, :, own]),
                (left, left_ref),
                (right, right_ref),
                (waves.at[0], ext.at[2, :, own]),
                (velocity, speeds.at[shot, own]),
            )
        )
    ]
    for load in loads:
        load.start()

    barrier = pltpu.get_barrier_semaphore()
    for side in range(2):
        @pl.when(has[side])
        def _():
            pl.semaphore_signal(barrier, inc=1, device_id={"space": beside[side]}, device_id_type=MESH)

    for ahead in range(1, shots):
        peer = lax.rem(shot + ahead, shots)
        pl.semaphore_signal(barrier, inc=1, device_id={"shot": peer}, device_id_type=MESH)
    pl.semaphore_wait(barrier, shots - 1 + jnp.where(has[0], 1, 0) + jnp.where(has[1], 1, 0))

    loads[0].wait()
    loads[4].wait()

    def message(source, target, slot, field, side):
        return pltpu.make_async_remote_copy(
            source,
            target,
            halo_send.at[slot, field, side],
            halo_recv.at[slot, field, 1 - side],
            device_id={"space": beside[side]},
            device_id_type=MESH,
        )

    def first_copy(field, side):
        return message(ext.at[0, field, border[side]], outer.at[STEPS - 2, field, 1 - side], 0, field, side)

    def second_copy(field, side):
        return message(ext.at[1, field, border[side]], ext.at[1, field, ghost[1 - side]], 1, field, side)

    def outer_copy(index, field, side):
        return message(
            ext.at[lax.rem(index, 3), field, beyond[side]],
            outer.at[index - 1, field, 1 - side],
            index + 1,
            field,
            side,
        )

    def rows_of(turn):
        chunk = lax.rem(shot * slab // tall + 1 + turn, chunks)
        return pl.ds(pl.multiple_of(chunk * tall, tall), tall)

    def last_copy(turn, field, side):
        rows = rows_of(turn)
        return message(
            ext.at[(last - 1) % 3, field, beyond[side], rows],
            outer.at[last - 2, field, 1 - side, :, rows],
            STEPS - 1 + turn,
            field,
            side,
        )

    def on_sides(act):
        for side in range(2):
            @pl.when(has[side])
            def _():
                act(side)

    def speed_copy(kind, side_or_span, ahead):
        return pltpu.make_async_remote_copy(
            speeds.at[shot, side_or_span],
            speeds.at[shot, side_or_span],
            speed_send.at[kind, ahead - 1],
            speed_recv.at[kind, ahead - 1],
            device_id={"shot": lax.rem(shot + ahead, shots)},
            device_id_type=MESH,
        )

    def next_speed(side):
        return pltpu.make_async_remote_copy(
            speeds.at[shot, border[side]],
            speeds.at[shot, ghost[1 - side]],
            speed_send.at[5, side],
            speed_recv.at[5, 1 - side],
            device_id={"space": beside[side]},
            device_id_type=MESH,
        )

    def ghost_speed(side, ahead):
        return pltpu.make_async_remote_copy(
            speeds.at[shot, ghost[side]],
            speeds.at[shot, ghost[side]],
            speed_send.at[3 + side, ahead - 1],
            speed_recv.at[3 + side, ahead - 1],
            device_id={"shot": lax.rem(shot + ahead, shots)},
            device_id_type=MESH,
        )

    spans = border + (inner,)
    on_sides(lambda side: first_copy(0, side).start())
    for kind in range(2):
        for ahead in range(1, shots):
            speed_copy(kind, spans[kind], ahead).start()
    on_sides(lambda side: first_copy(1, side).start())
    on_sides(lambda side: next_speed(side).start())
    for ahead in range(1, shots):
        speed_copy(2, spans[2], ahead).start()

    global_x = space * cells_x - REACH + lax.broadcasted_iota(jnp.int32, inside.shape, 0)
    seen = (global_x >= aperture[0, 0]) & (global_x < aperture[0, 1])
    inside[...] = jnp.where(seen, 1.0, 0.0)

    none = jnp.zeros((REACH, rows_y, rows_z), jnp.float32)
    for side in range(2):
        for field in range(2):
            ext[0, field, ghost[side]] = none

        @pl.when(jnp.logical_not(has[side]))
        def _():
            speed[ghost[side]] = none
            gain[ghost[side]] = none
            for field in range(2):
                ext[1, field, ghost[side]] = none

    def weigh(span):
        for index in range(shots):
            speed[span, index * slab : (index + 1) * slab, :] = speeds[index, span]
        scaled = speed[span] * inside[span] * (1.0 / SCALE)
        speed[span] = scaled
        gain[span] = 2.0 * inside[span] + CENTRE * scaled

    def gather(kind):
        for ahead in range(1, shots):
            speed_copy(kind, spans[kind], ahead).wait()
        weigh(spans[kind])

    def gather_ghost(side):
        for ahead in range(1, shots):
            ghost_speed(side, ahead).wait()
        weigh(ghost[side])

    def spread(now, field, span):
        cells = ext[now, field].reshape(flat)
        high = cells.astype(jnp.bfloat16)
        low = (cells - high.astype(jnp.float32)).astype(jnp.bfloat16)
        rows = slice(span.start * rows_y, span.stop * rows_y)
        return (
            jnp.dot(left_ref[rows], jnp.concatenate([high, low], axis=0), preferred_element_type=jnp.float32)
            + jnp.dot(
                jnp.concatenate([high[rows], low[rows]], axis=1), right_ref[...], preferred_element_type=jnp.float32
            )
        ).reshape((span.stop - span.start, rows_y, rows_z))

    def base(index, field, cells, around, masked=False):
        now, then, earlier = (lax.rem(index + ahead, 3) for ahead in range(3))
        before = ext[earlier, field, cells]
        if masked:
            before = inside[cells] * before
        ext[then, field, cells] = gain[cells] * ext[now, field, cells] - before + speed[cells] * around

    def correlate(then, cells):
        at = within(cells)
        total[at] = total[at] + ext[then, 0, cells] * ext[then, 1, cells]

    def terms(side, cell, layers):
        if side == 0:
            parts = [WEIGHTS[cell + REACH - layer] * layers[layer] for layer in range(cell, REACH)]
        else:
            parts = [WEIGHTS[REACH + layer - cell] * layers[layer] for layer in range(cell + 1)]
        return sum(parts[1:], parts[0])

    def added(slot, field, side, target, rows):
        layers = [outer[slot, field, side, layer, rows] for layer in range(REACH)]
        return [speed[target.start + cell, rows] * terms(side, cell, layers) for cell in range(REACH)]

    def put(then, field, target, rows, more):
        for cell in range(REACH):
            at = target.start + cell
            ext[then, field, at, rows] = ext[then, field, at, rows] + more[cell]

    every = slice(0, rows_y)

    def arrive(index, then, field):
        def act(side):
            outer_copy(index, field, 1 - side).wait_recv()
            put(then, field, ghost[side], every, added(index - 1, field, side, ghost[side], every))
        on_sides(act)

    for at in range(1, 3):
        loads[at].wait()

    def hand_on(side):
        next_speed(1 - side).wait_recv()
        for ahead in range(1, shots):
            ghost_speed(side, ahead).start()

    for field in range(2):
        lap[field, own] = spread(0, field, own)
    loads[3].wait()
    for kind in range(2):
        gather(kind)
        for field in range(2):
            base(0, field, border[kind], lap[field, border[kind]], True)

    def second(field):
        def act(side):
            first_copy(field, 1 - side).wait_recv()
            put(1, field, border[side], every, added(STEPS - 2, field, side, border[side], every))
            second_copy(field, side).start()
        on_sides(act)

    for field in range(2):
        second(field)
    on_sides(hand_on)
    gather(2)
    for field in range(2):
        base(0, field, inner, lap[field, inner], True)
        on_sides(lambda side: outer_copy(1, field, side).start())

    def settle(side):
        for field in range(2):
            ext[0, field, ghost[side]] = outer[STEPS - 2, field, side]

    on_sides(settle)
    total[...] = ext[1, 0, own] * ext[1, 1, own]
    on_sides(gather_ghost)

    everything = slice(0, wide)
    for field in range(2):
        on_sides(lambda side: second_copy(field, 1 - side).wait_recv())
        base(1, field, everything, spread(1, field, everything), True)
        on_sides(lambda side: outer_copy(2, field, side).start())
    correlate(2, own)
    for field in range(2):
        on_sides(lambda side: first_copy(field, side).wait_send())
        on_sides(lambda side: second_copy(field, side).wait_send())

    def step(index, carry):
        now = lax.rem(index, 3)
        for field in range(2):
            arrive(index - 1, now, field)

            @pl.when(index > 2)
            def _():
                on_sides(lambda side: outer_copy(index - 2, field, side).wait_send())

            base(index, field, everything, spread(now, field, everything))

            @pl.when(index < last - 2)
            def _():
                on_sides(lambda side: outer_copy(index + 1, field, side).start())

            @pl.when(index == last - 2)
            def _():
                if field == 0:
                    on_sides(lambda side: last_copy(0, 0, side).start())
                else:
                    on_sides(lambda side: last_copy(0, 1, side).start())
                    for turn in range(1, chunks):
                        for late in range(2):
                            on_sides(lambda side: last_copy(turn, late, side).start())

        correlate(lax.rem(index + 1, 3), own)
        return carry

    lax.fori_loop(2, last - 1, step, 0)

    then = STEPS % 3

    def part_copy(kind, source, target, ahead):
        peer = lax.rem(shot + ahead, shots)
        return pltpu.make_async_remote_copy(
            source.at[peer],
            target.at[ahead - 1],
            part_send.at[kind, ahead - 1],
            part_recv.at[kind, ahead - 1],
            device_id={"shot": peer},
            device_id_type=MESH,
        )

    for field in range(2):
        arrive(last - 2, (last - 1) % 3, field)
        on_sides(lambda side: outer_copy(last - 3, field, side).wait_send())
        base(last - 1, field, everything, spread((last - 1) % 3, field, everything))
        on_sides(lambda side: outer_copy(last - 2, field, side).wait_send())
        for span in (inner,) + border * (1 - field):
            base(last, field, span, spread(last % 3, field, span))
    correlate(last % 3, inner)
    correlate(then, inner)
    for index in range(shots):
        middle[index] = total[within(inner), index * slab : (index + 1) * slab, :]
    copies = [part_copy(0, middle, middle_arrived, ahead) for ahead in range(1, shots)]
    for copy in copies:
        copy.start()

    for span in border:
        correlate(last % 3, span)
        base(last, 1, span, spread(last % 3, 1, span))

    def complete(turn, field):
        rows = rows_of(turn)

        def act(side):
            last_copy(turn, field, 1 - side).wait_recv()
            layers = added(last - 2, field, side, ghost[side], rows)
            more = [speed[border[side].start + cell, rows] * terms(side, cell, layers) for cell in range(REACH)]
            put(then, field, border[side], rows, more)

        on_sides(act)

    for turn in range(chunks):
        for field in range(2):
            complete(turn, field)
        rows = rows_of(turn)
        chunk = lax.rem(shot * slab // tall + 1 + turn, chunks)
        for side in range(2):
            span = border[side]
            value = total[within(span), rows] + ext[then, 0, span, rows] * ext[then, 1, span, rows]
            for index in range(owners):
                edges[chunk * owners + index, side * REACH : (side + 1) * REACH] = value[
                    :, index * slab : (index + 1) * slab
                ]
        for index in range(owners):
            peer = chunk * owners + index

            @pl.when(peer != shot)
            def _():
                part_copy(1, edges, edges_arrived, lax.rem(peer - shot + shots, shots)).start()

    edge_copies = [part_copy(1, edges, edges_arrived, ahead) for ahead in range(1, shots)]

    def close(side):
        next_speed(side).wait_send()
        for field in range(2):
            for turn in range(chunks):
                last_copy(turn, field, side).wait_send()

    on_sides(close)
    summed = middle[shot]
    for copy, ahead in zip(copies, range(1, shots)):
        copy.wait()
        summed = summed + middle_arrived[ahead - 1]
    image[within(inner)] = summed / STEPS
    summed = edges[shot]
    for copy, ahead in zip(edge_copies, range(1, shots)):
        copy.wait()
        summed = summed + edges_arrived[ahead - 1]
    for side in range(2):
        image[within(border[side])] = summed[side * REACH : (side + 1) * REACH] / STEPS


def keep(ext, image, fields_out, image_out, store_sem):
    cells_x = fields_out.shape[2]
    stores = [pltpu.make_async_copy(image, image_out, store_sem.at[0])] + [
        pltpu.make_async_copy(ext.at[(STEPS - 1 + time) % 3, :, REACH : REACH + cells_x], fields_out.at[time], store_sem.at[1 + time])
        for time in range(2)
    ]
    for store in stores:
        store.start()
    for store in stores:
        store.wait()


def shards(wavefields, velocity, aperture):
    fields = wavefields[0]
    cells_x, rows_y, rows_z = fields.shape[2:]
    wide = cells_x + 2 * REACH
    shots = lax.axis_size("shot")
    slab = velocity.shape[1]
    chunks = max(rows_y // max(8, slab), 1)
    across = np.kron(band(wide), np.eye(rows_y, dtype=np.float32)) + np.kron(
        np.eye(wide, dtype=np.float32), band(rows_y)
    )
    left = np.concatenate([across, across], axis=1).astype(jnp.bfloat16)
    right = np.concatenate([band(rows_z)] * 2, axis=0).astype(jnp.bfloat16)
    grid = (wide, rows_y, rows_z)
    vmem = pl.BlockSpec(memory_space=pltpu.VMEM)
    anywhere = pl.BlockSpec(memory_space=pl.ANY)
    ext, image = pl.pallas_call(
        kernel,
        out_shape=(pltpu.VMEM((3, 2) + grid, jnp.float32), pltpu.VMEM(velocity.shape, jnp.float32)),
        in_specs=[anywhere, anywhere, anywhere, anywhere, pl.BlockSpec(memory_space=pltpu.SMEM)],
        out_specs=(vmem, vmem),
        scratch_shapes=[
            pltpu.VMEM(left.shape, jnp.bfloat16),
            pltpu.VMEM(right.shape, jnp.bfloat16),
            pltpu.VMEM((STEPS - 1, 2, 2, REACH, rows_y, rows_z), jnp.float32),
            pltpu.VMEM((shots, wide, slab, rows_z), jnp.float32),
            pltpu.VMEM(grid, jnp.float32),
            pltpu.VMEM(grid, jnp.float32),
            pltpu.VMEM(grid, jnp.float32),
            pltpu.VMEM((2,) + grid, jnp.float32),
            pltpu.VMEM((cells_x, rows_y, rows_z), jnp.float32),
            pltpu.VMEM((shots, cells_x - 2 * REACH, slab, rows_z), jnp.float32),
            pltpu.VMEM((shots - 1, cells_x - 2 * REACH, slab, rows_z), jnp.float32),
            pltpu.VMEM((shots, 2 * REACH, slab, rows_z), jnp.float32),
            pltpu.VMEM((shots - 1, 2 * REACH, slab, rows_z), jnp.float32),
            pltpu.SemaphoreType.DMA((STEPS - 1 + chunks, 2, 2)),
            pltpu.SemaphoreType.DMA((STEPS - 1 + chunks, 2, 2)),
            pltpu.SemaphoreType.DMA((6, max(shots - 1, 2))),
            pltpu.SemaphoreType.DMA((6, max(shots - 1, 2))),
            pltpu.SemaphoreType.DMA((2, shots - 1)),
            pltpu.SemaphoreType.DMA((2, shots - 1)),
            pltpu.SemaphoreType.DMA((5,)),
        ],
        compiler_params=pltpu.CompilerParams(collective_id=0, has_side_effects=True),
    )(jnp.asarray(left), jnp.asarray(right), fields, velocity, aperture)
    finals, image = pl.pallas_call(
        keep,
        out_shape=(
            jax.ShapeDtypeStruct(fields.shape, jnp.float32),
            jax.ShapeDtypeStruct(velocity.shape, jnp.float32),
        ),
        in_specs=[vmem, vmem],
        out_specs=(anywhere, anywhere),
        scratch_shapes=[pltpu.SemaphoreType.DMA((3,))],
    )(
        pltpu.with_memory_space_constraint(ext, pltpu.VMEM),
        pltpu.with_memory_space_constraint(image, pltpu.VMEM),
    )
    return finals[None], image


def solution(mesh):
    in_specs = (
        P(("groups", "shot"), None, None, "space", None, None),
        P(("groups", "space"), "shot", None),
        P(("groups", "shot"), None),
    )
    out_specs = (
        P(("groups", "shot"), None, None, "space", None, None),
        P(("groups", "space"), "shot", None),
    )
    return jax.shard_map(shards, mesh=mesh, in_specs=in_specs, out_specs=out_specs, check_vma=False)
```

```python
import functools

import jax
import jax.numpy as jnp
import numpy as np
from jax import lax
from jax.experimental import pallas as pl
from jax.experimental.pallas import tpu as pltpu
from jax.sharding import PartitionSpec as P

STEPS = 8
REACH = 4


SCALE = 5040.0
CENTRE = -3.0 * 14350.0
WEIGHTS = (0.0, 8064.0, -1008.0, 128.0, -9.0)
MESH = pl.DeviceIdType.MESH


def band(size):
    matrix = np.zeros((size, size), np.float32)
    for reach in range(1, REACH + 1):
        matrix += np.float32(WEIGHTS[reach]) * (
            np.eye(size, k=reach, dtype=np.float32) + np.eye(size, k=-reach, dtype=np.float32)
        )
    return matrix


def kernel(
    left, right, waves, velocity, aperture, ext, image,
    bounds, left_ref, right_ref, outer, speeds, speed, gain, inside, lap, total,
    middle, middle_arrived, edges, edges_arrived,
    halo_send, halo_recv, speed_send, speed_recv, part_send, part_recv, local_sem,
):
    space = lax.axis_index("space")
    spaces = lax.axis_size("space")
    shot = lax.axis_index("shot")
    shots = lax.axis_size("shot")
    wide, rows_y, rows_z = ext.shape[2:]
    cells_x, slab = velocity.shape[:2]
    flat = (wide * rows_y, rows_z)
    own = slice(REACH, REACH + cells_x)
    ghost = (slice(0, REACH), slice(wide - REACH, wide))
    border = (slice(REACH, 2 * REACH), slice(wide - 2 * REACH, wide - REACH))
    beyond = (slice(2 * REACH, 3 * REACH), slice(wide - 3 * REACH, wide - 2 * REACH))
    inner = slice(2 * REACH, wide - 2 * REACH)
    last = STEPS - 1
    chunks = halo_send.shape[0] - STEPS + 1
    tall = rows_y // chunks
    owners = shots // chunks
    has = (space > 0, space < spaces - 1)
    beside = (space - 1, space + 1)

    def within(span):
        return slice(span.start - REACH, span.stop - REACH)

    loads = [
        pltpu.make_async_copy(source, target, local_sem.at[at])
        for at, (source, target) in enumerate(
            (
                (waves.at[1], ext.at[0, :, own]),
                (left, left_ref),
                (right, right_ref),
                (waves.at[0], ext.at[2, :, own]),
                (velocity, speeds.at[shot, own]),
                (aperture, bounds),
            )
        )
    ]
    barrier = pltpu.get_barrier_semaphore()
    for side in range(2):
        @pl.when(has[side])
        def _():
            pl.semaphore_signal(barrier, inc=1, device_id={"space": beside[side]}, device_id_type=MESH)

    for ahead in range(1, shots):
        peer = lax.rem(shot + ahead, shots)
        pl.semaphore_signal(barrier, inc=1, device_id={"shot": peer}, device_id_type=MESH)
    for load in loads:
        load.start()

    pl.semaphore_wait(barrier, shots - 1 + jnp.where(has[0], 1, 0) + jnp.where(has[1], 1, 0))

    loads[0].wait()
    loads[4].wait()

    def message(source, target, slot, field, side):
        return pltpu.make_async_remote_copy(
            source,
            target,
            halo_send.at[slot, field, side],
            halo_recv.at[slot, field, 1 - side],
            device_id={"space": beside[side]},
            device_id_type=MESH,
        )

    def first_copy(field, side):
        return message(ext.at[0, field, border[side]], outer.at[STEPS - 2, field, 1 - side], 0, field, side)

    def second_copy(field, side):
        return message(ext.at[1, field, border[side]], ext.at[1, field, ghost[1 - side]], 1, field, side)

    def outer_copy(index, field, side):
        return message(
            ext.at[lax.rem(index, 3), field, beyond[side]],
            outer.at[index - 1, field, 1 - side],
            index + 1,
            field,
            side,
        )

    def rows_of(turn):
        chunk = lax.rem(shot * slab // tall + 1 + turn, chunks)
        return pl.ds(pl.multiple_of(chunk * tall, tall), tall)

    def last_copy(turn, field, side):
        rows = rows_of(turn)
        return message(
            ext.at[(last - 1) % 3, field, beyond[side], rows],
            outer.at[last - 2, field, 1 - side, :, rows],
            STEPS - 1 + turn,
            field,
            side,
        )

    def on_sides(act):
        for side in range(2):
            @pl.when(has[side])
            def _():
                act(side)

    def speed_copy(kind, side_or_span, ahead):
        return pltpu.make_async_remote_copy(
            speeds.at[shot, side_or_span],
            speeds.at[shot, side_or_span],
            speed_send.at[kind, ahead - 1],
            speed_recv.at[kind, ahead - 1],
            device_id={"shot": lax.rem(shot + ahead, shots)},
            device_id_type=MESH,
        )

    def next_speed(side):
        return pltpu.make_async_remote_copy(
            speeds.at[shot, border[side]],
            speeds.at[shot, ghost[1 - side]],
            speed_send.at[5, side],
            speed_recv.at[5, 1 - side],
            device_id={"space": beside[side]},
            device_id_type=MESH,
        )

    def ghost_speed(side, ahead):
        return pltpu.make_async_remote_copy(
            speeds.at[shot, ghost[side]],
            speeds.at[shot, ghost[side]],
            speed_send.at[3 + side, ahead - 1],
            speed_recv.at[3 + side, ahead - 1],
            device_id={"shot": lax.rem(shot + ahead, shots)},
            device_id_type=MESH,
        )

    spans = border + (inner,)
    on_sides(lambda side: first_copy(0, side).start())
    for kind in range(2):
        for ahead in range(1, shots):
            speed_copy(kind, spans[kind], ahead).start()
    on_sides(lambda side: first_copy(1, side).start())
    on_sides(lambda side: next_speed(side).start())
    for ahead in range(1, shots):
        speed_copy(2, spans[2], ahead).start()

    global_x = space * cells_x - REACH + lax.broadcasted_iota(jnp.int32, inside.shape, 0)
    loads[5].wait()
    seen = (global_x >= bounds[0, 0]) & (global_x < bounds[0, 1])
    inside[...] = jnp.where(seen, 1.0, 0.0)

    none = jnp.zeros((REACH, rows_y, rows_z), jnp.float32)
    for side in range(2):
        for field in range(2):
            ext[0, field, ghost[side]] = none

        @pl.when(jnp.logical_not(has[side]))
        def _():
            speed[ghost[side]] = none
            gain[ghost[side]] = none
            for field in range(2):
                ext[1, field, ghost[side]] = none

    def weigh(span):
        for index in range(shots):
            speed[span, index * slab : (index + 1) * slab, :] = speeds[index, span]
        scaled = speed[span] * inside[span] * (1.0 / SCALE)
        speed[span] = scaled
        gain[span] = 2.0 * inside[span] + CENTRE * scaled

    def gather(kind):
        for ahead in range(1, shots):
            speed_copy(kind, spans[kind], ahead).wait()
        weigh(spans[kind])

    def gather_ghost(side):
        for ahead in range(1, shots):
            ghost_speed(side, ahead).wait()
        weigh(ghost[side])

    def spread(now, field, span):
        cells = ext[now, field].reshape(flat)
        high = cells.astype(jnp.bfloat16)
        low = (cells - high.astype(jnp.float32)).astype(jnp.bfloat16)
        rows = slice(span.start * rows_y, span.stop * rows_y)
        return (
            jnp.dot(left_ref[rows], jnp.concatenate([high, low], axis=0), preferred_element_type=jnp.float32)
            + jnp.dot(
                jnp.concatenate([high[rows], low[rows]], axis=1), right_ref[...], preferred_element_type=jnp.float32
            )
        ).reshape((span.stop - span.start, rows_y, rows_z))

    def base(index, field, cells, around, masked=False):
        now, then, earlier = (lax.rem(index + ahead, 3) for ahead in range(3))
        before = ext[earlier, field, cells]
        if masked:
            before = inside[cells] * before
        ext[then, field, cells] = gain[cells] * ext[now, field, cells] - before + speed[cells] * around

    def correlate(then, cells):
        at = within(cells)
        total[at] = total[at] + ext[then, 0, cells] * ext[then, 1, cells]

    def terms(side, cell, layers):
        if side == 0:
            parts = [WEIGHTS[cell + REACH - layer] * layers[layer] for layer in range(cell, REACH)]
        else:
            parts = [WEIGHTS[REACH + layer - cell] * layers[layer] for layer in range(cell + 1)]
        return sum(parts[1:], parts[0])

    def added(slot, field, side, target, rows):
        layers = [outer[slot, field, side, layer, rows] for layer in range(REACH)]
        return [speed[target.start + cell, rows] * terms(side, cell, layers) for cell in range(REACH)]

    def put(then, field, target, rows, more):
        for cell in range(REACH):
            at = target.start + cell
            ext[then, field, at, rows] = ext[then, field, at, rows] + more[cell]

    every = slice(0, rows_y)

    def arrive(index, then, field):
        def act(side):
            outer_copy(index, field, 1 - side).wait_recv()
            put(then, field, ghost[side], every, added(index - 1, field, side, ghost[side], every))
        on_sides(act)

    for at in range(1, 3):
        loads[at].wait()

    def hand_on(side):
        next_speed(1 - side).wait_recv()
        for ahead in range(1, shots):
            ghost_speed(side, ahead).start()

    for field in range(2):
        lap[field, own] = spread(0, field, own)
    loads[3].wait()
    for kind in range(2):
        gather(kind)
        for field in range(2):
            base(0, field, border[kind], lap[field, border[kind]], True)

    def second(field):
        def act(side):
            first_copy(field, 1 - side).wait_recv()
            put(1, field, border[side], every, added(STEPS - 2, field, side, border[side], every))
            second_copy(field, side).start()
        on_sides(act)

    for field in range(2):
        second(field)
    on_sides(hand_on)
    gather(2)
    for field in range(2):
        base(0, field, inner, lap[field, inner], True)
        on_sides(lambda side: outer_copy(1, field, side).start())

    def settle(side):
        for field in range(2):
            ext[0, field, ghost[side]] = outer[STEPS - 2, field, side]

    on_sides(settle)
    total[...] = ext[1, 0, own] * ext[1, 1, own]
    on_sides(gather_ghost)

    everything = slice(0, wide)
    for field in range(2):
        on_sides(lambda side: second_copy(field, 1 - side).wait_recv())
        base(1, field, everything, spread(1, field, everything), True)
        on_sides(lambda side: outer_copy(2, field, side).start())
    correlate(2, own)
    for field in range(2):
        on_sides(lambda side: first_copy(field, side).wait_send())
        on_sides(lambda side: second_copy(field, side).wait_send())

    def step(index, carry):
        now = lax.rem(index, 3)
        for field in range(2):
            arrive(index - 1, now, field)

            @pl.when(index > 2)
            def _():
                on_sides(lambda side: outer_copy(index - 2, field, side).wait_send())

            base(index, field, everything, spread(now, field, everything))

            @pl.when(index < last - 2)
            def _():
                on_sides(lambda side: outer_copy(index + 1, field, side).start())

            @pl.when(index == last - 2)
            def _():
                if field == 0:
                    on_sides(lambda side: last_copy(0, 0, side).start())
                else:
                    on_sides(lambda side: last_copy(0, 1, side).start())
                    for turn in range(1, chunks):
                        for late in range(2):
                            on_sides(lambda side: last_copy(turn, late, side).start())

        correlate(lax.rem(index + 1, 3), own)
        return carry

    lax.fori_loop(2, last - 1, step, 0)

    then = STEPS % 3

    def part_copy(kind, source, target, ahead):
        peer = lax.rem(shot + ahead, shots)
        return pltpu.make_async_remote_copy(
            source.at[peer],
            target.at[ahead - 1],
            part_send.at[kind, ahead - 1],
            part_recv.at[kind, ahead - 1],
            device_id={"shot": peer},
            device_id_type=MESH,
        )

    for field in range(2):
        arrive(last - 2, (last - 1) % 3, field)
        on_sides(lambda side: outer_copy(last - 3, field, side).wait_send())
        base(last - 1, field, everything, spread((last - 1) % 3, field, everything))
        on_sides(lambda side: outer_copy(last - 2, field, side).wait_send())
        for span in (inner,) + border * (1 - field):
            base(last, field, span, spread(last % 3, field, span))
    correlate(last % 3, inner)
    correlate(then, inner)
    for index in range(shots):
        middle[index] = total[within(inner), index * slab : (index + 1) * slab, :]
    copies = [part_copy(0, middle, middle_arrived, ahead) for ahead in range(1, shots)]
    for copy in copies:
        copy.start()

    for span in border:
        correlate(last % 3, span)
        base(last, 1, span, spread(last % 3, 1, span))

    def complete(turn, field):
        rows = rows_of(turn)

        def act(side):
            last_copy(turn, field, 1 - side).wait_recv()
            layers = added(last - 2, field, side, ghost[side], rows)
            more = [speed[border[side].start + cell, rows] * terms(side, cell, layers) for cell in range(REACH)]
            put(then, field, border[side], rows, more)

        on_sides(act)

    for turn in range(chunks):
        for field in range(2):
            complete(turn, field)
        rows = rows_of(turn)
        chunk = lax.rem(shot * slab // tall + 1 + turn, chunks)
        for side in range(2):
            span = border[side]
            value = total[within(span), rows] + ext[then, 0, span, rows] * ext[then, 1, span, rows]
            for index in range(owners):
                edges[chunk * owners + index, side * REACH : (side + 1) * REACH] = value[
                    :, index * slab : (index + 1) * slab
                ]
        for index in range(owners):
            peer = chunk * owners + index

            @pl.when(peer != shot)
            def _():
                part_copy(1, edges, edges_arrived, lax.rem(peer - shot + shots, shots)).start()

    edge_copies = [part_copy(1, edges, edges_arrived, ahead) for ahead in range(1, shots)]

    def close(side):
        next_speed(side).wait_send()
        for field in range(2):
            for turn in range(chunks):
                last_copy(turn, field, side).wait_send()

    on_sides(close)
    summed = middle[shot]
    for copy, ahead in zip(copies, range(1, shots)):
        copy.wait()
        summed = summed + middle_arrived[ahead - 1]
    image[within(inner)] = summed / STEPS
    summed = edges[shot]
    for copy, ahead in zip(edge_copies, range(1, shots)):
        copy.wait()
        summed = summed + edges_arrived[ahead - 1]
    for side in range(2):
        image[within(border[side])] = summed[side * REACH : (side + 1) * REACH] / STEPS


def keep(ext, image, fields_out, image_out, store_sem):
    cells_x = fields_out.shape[2]
    stores = [pltpu.make_async_copy(image, image_out, store_sem.at[0])] + [
        pltpu.make_async_copy(ext.at[(STEPS - 1 + time) % 3, :, REACH : REACH + cells_x], fields_out.at[time], store_sem.at[1 + time])
        for time in range(2)
    ]
    for store in stores:
        store.start()
    for store in stores:
        store.wait()


def shards(wavefields, velocity, aperture):
    fields = wavefields[0]
    cells_x, rows_y, rows_z = fields.shape[2:]
    wide = cells_x + 2 * REACH
    shots = lax.axis_size("shot")
    slab = velocity.shape[1]
    chunks = max(rows_y // max(8, slab), 1)
    across = np.kron(band(wide), np.eye(rows_y, dtype=np.float32)) + np.kron(
        np.eye(wide, dtype=np.float32), band(rows_y)
    )
    left = np.concatenate([across, across], axis=1).astype(jnp.bfloat16)
    right = np.concatenate([band(rows_z)] * 2, axis=0).astype(jnp.bfloat16)
    grid = (wide, rows_y, rows_z)
    vmem = pl.BlockSpec(memory_space=pltpu.VMEM)
    anywhere = pl.BlockSpec(memory_space=pl.ANY)
    ext, image = pl.pallas_call(
        kernel,
        out_shape=(pltpu.VMEM((3, 2) + grid, jnp.float32), pltpu.VMEM(velocity.shape, jnp.float32)),
        in_specs=[anywhere] * 5,
        out_specs=(vmem, vmem),
        scratch_shapes=[
            pltpu.SMEM(aperture.shape, jnp.int32),
            pltpu.VMEM(left.shape, jnp.bfloat16),
            pltpu.VMEM(right.shape, jnp.bfloat16),
            pltpu.VMEM((STEPS - 1, 2, 2, REACH, rows_y, rows_z), jnp.float32),
            pltpu.VMEM((shots, wide, slab, rows_z), jnp.float32),
            pltpu.VMEM(grid, jnp.float32),
            pltpu.VMEM(grid, jnp.float32),
            pltpu.VMEM(grid, jnp.float32),
            pltpu.VMEM((2,) + grid, jnp.float32),
            pltpu.VMEM((cells_x, rows_y, rows_z), jnp.float32),
            pltpu.VMEM((shots, cells_x - 2 * REACH, slab, rows_z), jnp.float32),
            pltpu.VMEM((shots - 1, cells_x - 2 * REACH, slab, rows_z), jnp.float32),
            pltpu.VMEM((shots, 2 * REACH, slab, rows_z), jnp.float32),
            pltpu.VMEM((shots - 1, 2 * REACH, slab, rows_z), jnp.float32),
            pltpu.SemaphoreType.DMA((STEPS - 1 + chunks, 2, 2)),
            pltpu.SemaphoreType.DMA((STEPS - 1 + chunks, 2, 2)),
            pltpu.SemaphoreType.DMA((6, max(shots - 1, 2))),
            pltpu.SemaphoreType.DMA((6, max(shots - 1, 2))),
            pltpu.SemaphoreType.DMA((2, shots - 1)),
            pltpu.SemaphoreType.DMA((2, shots - 1)),
            pltpu.SemaphoreType.DMA((6,)),
        ],
        compiler_params=pltpu.CompilerParams(collective_id=0, has_side_effects=True),
    )(jnp.asarray(left), jnp.asarray(right), fields, velocity, aperture)
    finals, image = pl.pallas_call(
        keep,
        out_shape=(
            jax.ShapeDtypeStruct(fields.shape, jnp.float32),
            jax.ShapeDtypeStruct(velocity.shape, jnp.float32),
        ),
        in_specs=[vmem, vmem],
        out_specs=(anywhere, anywhere),
        scratch_shapes=[pltpu.SemaphoreType.DMA((3,))],
    )(
        pltpu.with_memory_space_constraint(ext, pltpu.VMEM),
        pltpu.with_memory_space_constraint(image, pltpu.VMEM),
    )
    return finals[None], image


def solution(mesh):
    in_specs = (
        P(("groups", "shot"), None, None, "space", None, None),
        P(("groups", "space"), "shot", None),
        P(("groups", "shot"), None),
    )
    out_specs = (
        P(("groups", "shot"), None, None, "space", None, None),
        P(("groups", "space"), "shot", None),
    )
    return jax.shard_map(shards, mesh=mesh, in_specs=in_specs, out_specs=out_specs, check_vma=False)
```

```python
import functools

import jax
import jax.numpy as jnp
import numpy as np
from jax import lax
from jax.experimental import pallas as pl
from jax.experimental.pallas import tpu as pltpu
from jax.sharding import PartitionSpec as P

STEPS = 8
REACH = 4


SCALE = 5040.0
CENTRE = -3.0 * 14350.0
WEIGHTS = (0.0, 8064.0, -1008.0, 128.0, -9.0)
MESH = pl.DeviceIdType.MESH


def band(size):
    matrix = np.zeros((size, size), np.float32)
    for reach in range(1, REACH + 1):
        matrix += np.float32(WEIGHTS[reach]) * (
            np.eye(size, k=reach, dtype=np.float32) + np.eye(size, k=-reach, dtype=np.float32)
        )
    return matrix


def kernel(
    left, right, waves, velocity, aperture, ext, image,
    bounds, left_ref, right_ref, outer, speeds, speed, gain, inside, lap, total,
    middle, middle_arrived, edges, edges_arrived,
    halo_send, halo_recv, speed_send, speed_recv, part_send, part_recv, local_sem,
):
    space = lax.axis_index("space")
    spaces = lax.axis_size("space")
    shot = lax.axis_index("shot")
    shots = lax.axis_size("shot")
    wide, rows_y, rows_z = ext.shape[2:]
    cells_x, slab = velocity.shape[:2]
    flat = (wide * rows_y, rows_z)
    own = slice(REACH, REACH + cells_x)
    ghost = (slice(0, REACH), slice(wide - REACH, wide))
    border = (slice(REACH, 2 * REACH), slice(wide - 2 * REACH, wide - REACH))
    beyond = (slice(2 * REACH, 3 * REACH), slice(wide - 3 * REACH, wide - 2 * REACH))
    inner = slice(2 * REACH, wide - 2 * REACH)
    last = STEPS - 1
    chunks = halo_send.shape[0] - STEPS + 1
    tall = rows_y // chunks
    owners = shots // chunks
    has = (space > 0, space < spaces - 1)
    beside = (space - 1, space + 1)

    def within(span):
        return slice(span.start - REACH, span.stop - REACH)

    loads = [
        pltpu.make_async_copy(source, target, local_sem.at[at])
        for at, (source, target) in enumerate(
            (
                (waves.at[1], ext.at[0, :, own]),
                (velocity, speeds.at[shot, own]),
                (aperture, bounds),
                (left, left_ref),
                (right, right_ref),
                (waves.at[0], ext.at[2, :, own]),
            )
        )
    ]
    barrier = pltpu.get_barrier_semaphore()
    for side in range(2):
        @pl.when(has[side])
        def _():
            pl.semaphore_signal(barrier, inc=1, device_id={"space": beside[side]}, device_id_type=MESH)

    for ahead in range(1, shots):
        peer = lax.rem(shot + ahead, shots)
        pl.semaphore_signal(barrier, inc=1, device_id={"shot": peer}, device_id_type=MESH)
    for load in loads:
        load.start()

    pl.semaphore_wait(barrier, shots - 1 + jnp.where(has[0], 1, 0) + jnp.where(has[1], 1, 0))

    loads[0].wait()

    def message(source, target, slot, field, side):
        return pltpu.make_async_remote_copy(
            source,
            target,
            halo_send.at[slot, field, side],
            halo_recv.at[slot, field, 1 - side],
            device_id={"space": beside[side]},
            device_id_type=MESH,
        )

    def first_copy(field, side):
        return message(ext.at[0, field, border[side]], outer.at[STEPS - 2, field, 1 - side], 0, field, side)

    def second_copy(field, side):
        return message(ext.at[1, field, border[side]], ext.at[1, field, ghost[1 - side]], 1, field, side)

    def outer_copy(index, field, side):
        return message(
            ext.at[lax.rem(index, 3), field, beyond[side]],
            outer.at[index - 1, field, 1 - side],
            index + 1,
            field,
            side,
        )

    def rows_of(turn):
        chunk = lax.rem(shot * slab // tall + 1 + turn, chunks)
        return pl.ds(pl.multiple_of(chunk * tall, tall), tall)

    def last_copy(turn, field, side):
        rows = rows_of(turn)
        return message(
            ext.at[(last - 1) % 3, field, beyond[side], rows],
            outer.at[last - 2, field, 1 - side, :, rows],
            STEPS - 1 + turn,
            field,
            side,
        )

    def on_sides(act):
        for side in range(2):
            @pl.when(has[side])
            def _():
                act(side)

    def speed_copy(kind, side_or_span, ahead):
        return pltpu.make_async_remote_copy(
            speeds.at[shot, side_or_span],
            speeds.at[shot, side_or_span],
            speed_send.at[kind, ahead - 1],
            speed_recv.at[kind, ahead - 1],
            device_id={"shot": lax.rem(shot + ahead, shots)},
            device_id_type=MESH,
        )

    def next_speed(side):
        return pltpu.make_async_remote_copy(
            speeds.at[shot, border[side]],
            speeds.at[shot, ghost[1 - side]],
            speed_send.at[5, side],
            speed_recv.at[5, 1 - side],
            device_id={"space": beside[side]},
            device_id_type=MESH,
        )

    def ghost_speed(side, ahead):
        return pltpu.make_async_remote_copy(
            speeds.at[shot, ghost[side]],
            speeds.at[shot, ghost[side]],
            speed_send.at[3 + side, ahead - 1],
            speed_recv.at[3 + side, ahead - 1],
            device_id={"shot": lax.rem(shot + ahead, shots)},
            device_id_type=MESH,
        )

    spans = border + (inner,)
    on_sides(lambda side: first_copy(0, side).start())
    loads[1].wait()
    for kind in range(2):
        for ahead in range(1, shots):
            speed_copy(kind, spans[kind], ahead).start()
    on_sides(lambda side: first_copy(1, side).start())
    on_sides(lambda side: next_speed(side).start())
    for ahead in range(1, shots):
        speed_copy(2, spans[2], ahead).start()

    global_x = space * cells_x - REACH + lax.broadcasted_iota(jnp.int32, inside.shape, 0)
    loads[2].wait()
    seen = (global_x >= bounds[0, 0]) & (global_x < bounds[0, 1])
    inside[...] = jnp.where(seen, 1.0, 0.0)

    none = jnp.zeros((REACH, rows_y, rows_z), jnp.float32)
    for side in range(2):
        for field in range(2):
            ext[0, field, ghost[side]] = none

        @pl.when(jnp.logical_not(has[side]))
        def _():
            speed[ghost[side]] = none
            gain[ghost[side]] = none
            for field in range(2):
                ext[1, field, ghost[side]] = none

    def weigh(span):
        for index in range(shots):
            speed[span, index * slab : (index + 1) * slab, :] = speeds[index, span]
        scaled = speed[span] * inside[span] * (1.0 / SCALE)
        speed[span] = scaled
        gain[span] = 2.0 * inside[span] + CENTRE * scaled

    def gather(kind):
        for ahead in range(1, shots):
            speed_copy(kind, spans[kind], ahead).wait()
        weigh(spans[kind])

    def gather_ghost(side):
        for ahead in range(1, shots):
            ghost_speed(side, ahead).wait()
        weigh(ghost[side])

    def spread(now, field, span):
        cells = ext[now, field].reshape(flat)
        high = cells.astype(jnp.bfloat16)
        low = (cells - high.astype(jnp.float32)).astype(jnp.bfloat16)
        rows = slice(span.start * rows_y, span.stop * rows_y)
        return (
            jnp.dot(left_ref[rows], jnp.concatenate([high, low], axis=0), preferred_element_type=jnp.float32)
            + jnp.dot(
                jnp.concatenate([high[rows], low[rows]], axis=1), right_ref[...], preferred_element_type=jnp.float32
            )
        ).reshape((span.stop - span.start, rows_y, rows_z))

    def base(index, field, cells, around, masked=False):
        now, then, earlier = (lax.rem(index + ahead, 3) for ahead in range(3))
        before = ext[earlier, field, cells]
        if masked:
            before = inside[cells] * before
        ext[then, field, cells] = gain[cells] * ext[now, field, cells] - before + speed[cells] * around

    def correlate(then, cells):
        at = within(cells)
        total[at] = total[at] + ext[then, 0, cells] * ext[then, 1, cells]

    def terms(side, cell, layers):
        if side == 0:
            parts = [WEIGHTS[cell + REACH - layer] * layers[layer] for layer in range(cell, REACH)]
        else:
            parts = [WEIGHTS[REACH + layer - cell] * layers[layer] for layer in range(cell + 1)]
        return sum(parts[1:], parts[0])

    def added(slot, field, side, target, rows):
        layers = [outer[slot, field, side, layer, rows] for layer in range(REACH)]
        return [speed[target.start + cell, rows] * terms(side, cell, layers) for cell in range(REACH)]

    def put(then, field, target, rows, more):
        for cell in range(REACH):
            at = target.start + cell
            ext[then, field, at, rows] = ext[then, field, at, rows] + more[cell]

    every = slice(0, rows_y)

    def arrive(index, then, field):
        def act(side):
            outer_copy(index, field, 1 - side).wait_recv()
            put(then, field, ghost[side], every, added(index - 1, field, side, ghost[side], every))
        on_sides(act)

    for at in range(3, 5):
        loads[at].wait()

    def hand_on(side):
        next_speed(1 - side).wait_recv()
        for ahead in range(1, shots):
            ghost_speed(side, ahead).start()

    for field in range(2):
        lap[field, own] = spread(0, field, own)
    loads[5].wait()
    for kind in range(2):
        gather(kind)
        for field in range(2):
            base(0, field, border[kind], lap[field, border[kind]], True)

    def second(field):
        def act(side):
            first_copy(field, 1 - side).wait_recv()
            put(1, field, border[side], every, added(STEPS - 2, field, side, border[side], every))
            second_copy(field, side).start()
        on_sides(act)

    for field in range(2):
        second(field)
    on_sides(hand_on)
    gather(2)
    for field in range(2):
        base(0, field, inner, lap[field, inner], True)
        on_sides(lambda side: outer_copy(1, field, side).start())

    def settle(side):
        for field in range(2):
            ext[0, field, ghost[side]] = outer[STEPS - 2, field, side]

    on_sides(settle)
    total[...] = ext[1, 0, own] * ext[1, 1, own]
    on_sides(gather_ghost)

    everything = slice(0, wide)
    for field in range(2):
        on_sides(lambda side: second_copy(field, 1 - side).wait_recv())
        base(1, field, everything, spread(1, field, everything), True)
        on_sides(lambda side: outer_copy(2, field, side).start())
    correlate(2, own)
    for field in range(2):
        on_sides(lambda side: first_copy(field, side).wait_send())
        on_sides(lambda side: second_copy(field, side).wait_send())

    def step(index, carry):
        now = lax.rem(index, 3)
        for field in range(2):
            arrive(index - 1, now, field)

            @pl.when(index > 2)
            def _():
                on_sides(lambda side: outer_copy(index - 2, field, side).wait_send())

            base(index, field, everything, spread(now, field, everything))

            @pl.when(index < last - 2)
            def _():
                on_sides(lambda side: outer_copy(index + 1, field, side).start())

            @pl.when((index == last - 2) & (lax.rem(shot, 2) == 0))
            def _():
                if field == 0:
                    on_sides(lambda side: last_copy(0, 0, side).start())
                else:
                    on_sides(lambda side: last_copy(0, 1, side).start())
                    for turn in range(1, chunks):
                        for late in range(2):
                            on_sides(lambda side: last_copy(turn, late, side).start())

        correlate(lax.rem(index + 1, 3), own)
        return carry

    lax.fori_loop(2, last - 1, step, 0)

    then = STEPS % 3

    def part_copy(kind, source, target, ahead):
        peer = lax.rem(shot + ahead, shots)
        return pltpu.make_async_remote_copy(
            source.at[peer],
            target.at[ahead - 1],
            part_send.at[kind, ahead - 1],
            part_recv.at[kind, ahead - 1],
            device_id={"shot": peer},
            device_id_type=MESH,
        )

    for field in range(2):
        if field == 0:
            @pl.when(lax.rem(shot, 2) == 1)
            def _():
                for turn in range(chunks):
                    for late in range(2):
                        on_sides(lambda side: last_copy(turn, late, side).start())

        arrive(last - 2, (last - 1) % 3, field)
        on_sides(lambda side: outer_copy(last - 3, field, side).wait_send())
        base(last - 1, field, everything, spread((last - 1) % 3, field, everything))
        on_sides(lambda side: outer_copy(last - 2, field, side).wait_send())
        for span in (inner,) + border * (1 - field):
            base(last, field, span, spread(last % 3, field, span))
    correlate(last % 3, inner)
    correlate(then, inner)
    for index in range(shots):
        middle[index] = total[within(inner), index * slab : (index + 1) * slab, :]
    copies = [part_copy(0, middle, middle_arrived, ahead) for ahead in range(1, shots)]
    for copy in copies[1:] + copies[:1]:
        copy.start()

    for span in border:
        correlate(last % 3, span)
        base(last, 1, span, spread(last % 3, 1, span))

    def complete(turn, field):
        rows = rows_of(turn)

        def act(side):
            last_copy(turn, field, 1 - side).wait_recv()
            layers = added(last - 2, field, side, ghost[side], rows)
            more = [speed[border[side].start + cell, rows] * terms(side, cell, layers) for cell in range(REACH)]
            put(then, field, border[side], rows, more)

        on_sides(act)

    for turn in range(chunks):
        for field in range(2):
            complete(turn, field)
        rows = rows_of(turn)
        chunk = lax.rem(shot * slab // tall + 1 + turn, chunks)
        for side in range(2):
            span = border[side]
            value = total[within(span), rows] + ext[then, 0, span, rows] * ext[then, 1, span, rows]
            for index in range(owners):
                edges[chunk * owners + index, side * REACH : (side + 1) * REACH] = value[
                    :, index * slab : (index + 1) * slab
                ]
        for index in range(owners):
            peer = chunk * owners + index

            @pl.when(peer != shot)
            def _():
                part_copy(1, edges, edges_arrived, lax.rem(peer - shot + shots, shots)).start()

    edge_copies = [part_copy(1, edges, edges_arrived, ahead) for ahead in range(1, shots)]

    def close(side):
        next_speed(side).wait_send()
        for field in range(2):
            for turn in range(chunks):
                last_copy(turn, field, side).wait_send()

    on_sides(close)
    summed = middle[shot]
    for copy, ahead in zip(copies, range(1, shots)):
        copy.wait()
        summed = summed + middle_arrived[ahead - 1]
    image[within(inner)] = summed / STEPS
    summed = edges[shot]
    for copy, ahead in zip(edge_copies, range(1, shots)):
        copy.wait()
        summed = summed + edges_arrived[ahead - 1]
    for side in range(2):
        image[within(border[side])] = summed[side * REACH : (side + 1) * REACH] / STEPS


def keep(ext, image, fields_out, image_out, store_sem):
    cells_x = fields_out.shape[2]
    stores = [pltpu.make_async_copy(image, image_out, store_sem.at[0])] + [
        pltpu.make_async_copy(ext.at[(STEPS - 1 + time) % 3, :, REACH : REACH + cells_x], fields_out.at[time], store_sem.at[1 + time])
        for time in range(2)
    ]
    for store in stores[::-1]:
        store.start()
    for store in stores:
        store.wait()


def shards(wavefields, velocity, aperture):
    fields = wavefields[0]
    cells_x, rows_y, rows_z = fields.shape[2:]
    wide = cells_x + 2 * REACH
    shots = lax.axis_size("shot")
    slab = velocity.shape[1]
    chunks = max(rows_y // max(8, slab), 1)
    across = np.kron(band(wide), np.eye(rows_y, dtype=np.float32)) + np.kron(
        np.eye(wide, dtype=np.float32), band(rows_y)
    )
    left = np.concatenate([across, across], axis=1).astype(jnp.bfloat16)
    right = np.concatenate([band(rows_z)] * 2, axis=0).astype(jnp.bfloat16)
    grid = (wide, rows_y, rows_z)
    vmem = pl.BlockSpec(memory_space=pltpu.VMEM)
    anywhere = pl.BlockSpec(memory_space=pl.ANY)
    ext, image = pl.pallas_call(
        kernel,
        out_shape=(pltpu.VMEM((3, 2) + grid, jnp.float32), pltpu.VMEM(velocity.shape, jnp.float32)),
        in_specs=[anywhere] * 5,
        out_specs=(vmem, vmem),
        scratch_shapes=[
            pltpu.SMEM(aperture.shape, jnp.int32),
            pltpu.VMEM(left.shape, jnp.bfloat16),
            pltpu.VMEM(right.shape, jnp.bfloat16),
            pltpu.VMEM((STEPS - 1, 2, 2, REACH, rows_y, rows_z), jnp.float32),
            pltpu.VMEM((shots, wide, slab, rows_z), jnp.float32),
            pltpu.VMEM(grid, jnp.float32),
            pltpu.VMEM(grid, jnp.float32),
            pltpu.VMEM(grid, jnp.float32),
            pltpu.VMEM((2,) + grid, jnp.float32),
            pltpu.VMEM((cells_x, rows_y, rows_z), jnp.float32),
            pltpu.VMEM((shots, cells_x - 2 * REACH, slab, rows_z), jnp.float32),
            pltpu.VMEM((shots - 1, cells_x - 2 * REACH, slab, rows_z), jnp.float32),
            pltpu.VMEM((shots, 2 * REACH, slab, rows_z), jnp.float32),
            pltpu.VMEM((shots - 1, 2 * REACH, slab, rows_z), jnp.float32),
            pltpu.SemaphoreType.DMA((STEPS - 1 + chunks, 2, 2)),
            pltpu.SemaphoreType.DMA((STEPS - 1 + chunks, 2, 2)),
            pltpu.SemaphoreType.DMA((6, max(shots - 1, 2))),
            pltpu.SemaphoreType.DMA((6, max(shots - 1, 2))),
            pltpu.SemaphoreType.DMA((2, shots - 1)),
            pltpu.SemaphoreType.DMA((2, shots - 1)),
            pltpu.SemaphoreType.DMA((6,)),
        ],
        compiler_params=pltpu.CompilerParams(collective_id=0, has_side_effects=True),
    )(jnp.asarray(left), jnp.asarray(right), fields, velocity, aperture)
    finals, image = pl.pallas_call(
        keep,
        out_shape=(
            jax.ShapeDtypeStruct(fields.shape, jnp.float32),
            jax.ShapeDtypeStruct(velocity.shape, jnp.float32),
        ),
        in_specs=[vmem, vmem],
        out_specs=(anywhere, anywhere),
        scratch_shapes=[pltpu.SemaphoreType.DMA((3,))],
    )(
        pltpu.with_memory_space_constraint(ext, pltpu.VMEM),
        pltpu.with_memory_space_constraint(image, pltpu.VMEM),
    )
    return finals[None], image


def solution(mesh):
    in_specs = (
        P(("groups", "shot"), None, None, "space", None, None),
        P(("groups", "space"), "shot", None),
        P(("groups", "shot"), None),
    )
    out_specs = (
        P(("groups", "shot"), None, None, "space", None, None),
        P(("groups", "space"), "shot", None),
    )
    return jax.shard_map(shards, mesh=mesh, in_specs=in_specs, out_specs=out_specs, check_vma=False)
```

```python
import functools

import jax
import jax.numpy as jnp
import numpy as np
from jax import lax
from jax.experimental import pallas as pl
from jax.experimental.pallas import tpu as pltpu
from jax.sharding import PartitionSpec as P

STEPS = 8
REACH = 4


SCALE = 5040.0
CENTRE = -3.0 * 14350.0
WEIGHTS = (0.0, 8064.0, -1008.0, 128.0, -9.0)
MESH = pl.DeviceIdType.MESH


def band(size):
    matrix = np.zeros((size, size), np.float32)
    for reach in range(1, REACH + 1):
        matrix += np.float32(WEIGHTS[reach]) * (
            np.eye(size, k=reach, dtype=np.float32) + np.eye(size, k=-reach, dtype=np.float32)
        )
    return matrix


def kernel(
    left, right, waves, velocity, aperture, ext, image,
    bounds, left_ref, right_ref, outer, speeds, speed, gain, inside, lap, total,
    middle, middle_arrived, edges, edges_arrived,
    halo_send, halo_recv, speed_send, speed_recv, part_send, part_recv, local_sem,
):
    space = lax.axis_index("space")
    spaces = lax.axis_size("space")
    shot = lax.axis_index("shot")
    shots = lax.axis_size("shot")
    wide, rows_y, rows_z = ext.shape[2:]
    cells_x, slab = velocity.shape[:2]
    flat = (wide * rows_y, rows_z)
    own = slice(REACH, REACH + cells_x)
    ghost = (slice(0, REACH), slice(wide - REACH, wide))
    border = (slice(REACH, 2 * REACH), slice(wide - 2 * REACH, wide - REACH))
    beyond = (slice(2 * REACH, 3 * REACH), slice(wide - 3 * REACH, wide - 2 * REACH))
    inner = slice(2 * REACH, wide - 2 * REACH)
    last = STEPS - 1
    chunks = halo_send.shape[0] - STEPS + 1
    tall = rows_y // chunks
    owners = shots // chunks
    has = (space > 0, space < spaces - 1)
    beside = (space - 1, space + 1)

    def within(span):
        return slice(span.start - REACH, span.stop - REACH)

    loads = [
        pltpu.make_async_copy(source, target, local_sem.at[at])
        for at, (source, target) in enumerate(
            (
                (waves.at[1], ext.at[0, :, own]),
                (left, left_ref),
                (right, right_ref),
                (waves.at[0], ext.at[2, :, own]),
                (velocity, speeds.at[shot, own]),
                (aperture, bounds),
            )
        )
    ]
    barrier = pltpu.get_barrier_semaphore()
    for side in range(2):
        @pl.when(has[side])
        def _():
            pl.semaphore_signal(barrier, inc=1, device_id={"space": beside[side]}, device_id_type=MESH)

    for ahead in range(1, shots):
        peer = lax.rem(shot + ahead, shots)
        pl.semaphore_signal(barrier, inc=1, device_id={"shot": peer}, device_id_type=MESH)
    for load in loads:
        load.start()

    pl.semaphore_wait(barrier, shots - 1 + jnp.where(has[0], 1, 0) + jnp.where(has[1], 1, 0))

    loads[0].wait()
    loads[4].wait()

    def message(source, target, slot, field, side):
        return pltpu.make_async_remote_copy(
            source,
            target,
            halo_send.at[slot, field, side],
            halo_recv.at[slot, field, 1 - side],
            device_id={"space": beside[side]},
            device_id_type=MESH,
        )

    def first_copy(field, side):
        return message(ext.at[0, field, border[side]], outer.at[STEPS - 2, field, 1 - side], 0, field, side)

    def second_copy(field, side):
        return message(ext.at[1, field, border[side]], ext.at[1, field, ghost[1 - side]], 1, field, side)

    def outer_copy(index, field, side):
        return message(
            ext.at[lax.rem(index, 3), field, beyond[side]],
            outer.at[index - 1, field, 1 - side],
            index + 1,
            field,
            side,
        )

    def rows_of(turn):
        chunk = lax.rem(shot * slab // tall + 1 + turn, chunks)
        return pl.ds(pl.multiple_of(chunk * tall, tall), tall)

    def last_copy(turn, field, side):
        rows = rows_of(turn)
        return message(
            ext.at[(last - 1) % 3, field, beyond[side], rows],
            outer.at[last - 2, field, 1 - side, :, rows],
            STEPS - 1 + turn,
            field,
            side,
        )

    odd = lax.rem(shot, 2)

    def send_sides(act):
        for side, mine in ((0, 0), (1, None), (0, 1)):
            @pl.when(has[side] if mine is None else has[side] & (odd == mine))
            def _():
                act(side)

    def on_sides(act):
        for side in range(2):
            @pl.when(has[side])
            def _():
                act(side)

    def speed_copy(kind, side_or_span, ahead):
        return pltpu.make_async_remote_copy(
            speeds.at[shot, side_or_span],
            speeds.at[shot, side_or_span],
            speed_send.at[kind, ahead - 1],
            speed_recv.at[kind, ahead - 1],
            device_id={"shot": lax.rem(shot + ahead, shots)},
            device_id_type=MESH,
        )

    def next_speed(side):
        return pltpu.make_async_remote_copy(
            speeds.at[shot, border[side]],
            speeds.at[shot, ghost[1 - side]],
            speed_send.at[5, side],
            speed_recv.at[5, 1 - side],
            device_id={"space": beside[side]},
            device_id_type=MESH,
        )

    def ghost_speed(side, ahead):
        return pltpu.make_async_remote_copy(
            speeds.at[shot, ghost[side]],
            speeds.at[shot, ghost[side]],
            speed_send.at[3 + side, ahead - 1],
            speed_recv.at[3 + side, ahead - 1],
            device_id={"shot": lax.rem(shot + ahead, shots)},
            device_id_type=MESH,
        )

    spans = border + (inner,)
    send_sides(lambda side: first_copy(0, side).start())
    for kind in range(2):
        for ahead in range(1, shots):
            speed_copy(kind, spans[kind], ahead).start()
    send_sides(lambda side: first_copy(1, side).start())
    on_sides(lambda side: next_speed(side).start())
    for ahead in range(1, shots):
        speed_copy(2, spans[2], ahead).start()

    global_x = space * cells_x - REACH + lax.broadcasted_iota(jnp.int32, inside.shape, 0)
    loads[5].wait()
    seen = (global_x >= bounds[0, 0]) & (global_x < bounds[0, 1])
    inside[...] = jnp.where(seen, 1.0, 0.0)

    none = jnp.zeros((REACH, rows_y, rows_z), jnp.float32)
    for side in range(2):
        for field in range(2):
            ext[0, field, ghost[side]] = none

        @pl.when(jnp.logical_not(has[side]))
        def _():
            speed[ghost[side]] = none
            gain[ghost[side]] = none
            for field in range(2):
                ext[1, field, ghost[side]] = none

    def weigh(span):
        for index in range(shots):
            speed[span, index * slab : (index + 1) * slab, :] = speeds[index, span]
        scaled = speed[span] * inside[span] * (1.0 / SCALE)
        speed[span] = scaled
        gain[span] = 2.0 * inside[span] + CENTRE * scaled

    def gather(kind):
        for ahead in range(1, shots):
            speed_copy(kind, spans[kind], ahead).wait()
        weigh(spans[kind])

    def gather_ghost(side):
        for ahead in range(1, shots):
            ghost_speed(side, ahead).wait()
        weigh(ghost[side])

    def spread(now, field, span):
        cells = ext[now, field].reshape(flat)
        high = cells.astype(jnp.bfloat16)
        low = (cells - high.astype(jnp.float32)).astype(jnp.bfloat16)
        rows = slice(span.start * rows_y, span.stop * rows_y)
        return (
            jnp.dot(left_ref[rows], jnp.concatenate([high, low], axis=0), preferred_element_type=jnp.float32)
            + jnp.dot(
                jnp.concatenate([high[rows], low[rows]], axis=1), right_ref[...], preferred_element_type=jnp.float32
            )
        ).reshape((span.stop - span.start, rows_y, rows_z))

    def base(index, field, cells, around, masked=False):
        now, then, earlier = (lax.rem(index + ahead, 3) for ahead in range(3))
        before = ext[earlier, field, cells]
        if masked:
            before = inside[cells] * before
        ext[then, field, cells] = gain[cells] * ext[now, field, cells] - before + speed[cells] * around

    def correlate(then, cells):
        at = within(cells)
        total[at] = total[at] + ext[then, 0, cells] * ext[then, 1, cells]

    def terms(side, cell, layers):
        if side == 0:
            parts = [WEIGHTS[cell + REACH - layer] * layers[layer] for layer in range(cell, REACH)]
        else:
            parts = [WEIGHTS[REACH + layer - cell] * layers[layer] for layer in range(cell + 1)]
        return sum(parts[1:], parts[0])

    def added(slot, field, side, target, rows):
        layers = [outer[slot, field, side, layer, rows] for layer in range(REACH)]
        return [speed[target.start + cell, rows] * terms(side, cell, layers) for cell in range(REACH)]

    def put(then, field, target, rows, more):
        for cell in range(REACH):
            at = target.start + cell
            ext[then, field, at, rows] = ext[then, field, at, rows] + more[cell]

    every = slice(0, rows_y)

    def arrive(index, then, field):
        def act(side):
            outer_copy(index, field, 1 - side).wait_recv()
            put(then, field, ghost[side], every, added(index - 1, field, side, ghost[side], every))
        on_sides(act)

    for at in range(1, 3):
        loads[at].wait()

    def hand_on(side):
        next_speed(1 - side).wait_recv()
        for ahead in range(1, shots):
            ghost_speed(side, ahead).start()

    for field in range(2):
        lap[field, own] = spread(0, field, own)
    loads[3].wait()
    for kind in range(2):
        gather(kind)
        for field in range(2):
            base(0, field, border[kind], lap[field, border[kind]], True)

    def second(field):
        def act(side):
            first_copy(field, 1 - side).wait_recv()
            put(1, field, border[side], every, added(STEPS - 2, field, side, border[side], every))
            second_copy(field, side).start()
        on_sides(act)

    for field in range(2):
        second(field)
    on_sides(hand_on)
    gather(2)
    for field in range(2):
        base(0, field, inner, lap[field, inner], True)
        send_sides(lambda side: outer_copy(1, field, side).start())

    def settle(side):
        for field in range(2):
            ext[0, field, ghost[side]] = outer[STEPS - 2, field, side]

    on_sides(settle)
    total[...] = ext[1, 0, own] * ext[1, 1, own]
    on_sides(gather_ghost)

    everything = slice(0, wide)
    for field in range(2):
        on_sides(lambda side: second_copy(field, 1 - side).wait_recv())
        base(1, field, everything, spread(1, field, everything), True)
        send_sides(lambda side: outer_copy(2, field, side).start())
    correlate(2, own)
    for field in range(2):
        on_sides(lambda side: first_copy(field, side).wait_send())
        on_sides(lambda side: second_copy(field, side).wait_send())

    def step(index, carry):
        now = lax.rem(index, 3)
        for field in range(2):
            arrive(index - 1, now, field)

            @pl.when(index > 2)
            def _():
                on_sides(lambda side: outer_copy(index - 2, field, side).wait_send())

            base(index, field, everything, spread(now, field, everything))

            @pl.when(index < last - 2)
            def _():
                send_sides(lambda side: outer_copy(index + 1, field, side).start())

            @pl.when(index == last - 2)
            def _():
                if field == 0:
                    send_sides(lambda side: last_copy(0, 0, side).start())
                else:
                    send_sides(lambda side: last_copy(0, 1, side).start())
                    for turn in range(1, chunks):
                        for late in range(2):
                            send_sides(lambda side: last_copy(turn, late, side).start())

        correlate(lax.rem(index + 1, 3), own)
        return carry

    lax.fori_loop(2, last - 1, step, 0)

    then = STEPS % 3

    def part_copy(kind, source, target, ahead):
        peer = lax.rem(shot + ahead, shots)
        return pltpu.make_async_remote_copy(
            source.at[peer],
            target.at[ahead - 1],
            part_send.at[kind, ahead - 1],
            part_recv.at[kind, ahead - 1],
            device_id={"shot": peer},
            device_id_type=MESH,
        )

    for field in range(2):
        arrive(last - 2, (last - 1) % 3, field)
        on_sides(lambda side: outer_copy(last - 3, field, side).wait_send())
        base(last - 1, field, everything, spread((last - 1) % 3, field, everything))
        on_sides(lambda side: outer_copy(last - 2, field, side).wait_send())
        for span in (inner,) + border * (1 - field):
            base(last, field, span, spread(last % 3, field, span))
    correlate(last % 3, inner)
    correlate(then, inner)
    for index in range(shots):
        middle[index] = total[within(inner), index * slab : (index + 1) * slab, :]
    copies = [part_copy(0, middle, middle_arrived, ahead) for ahead in range(1, shots)]
    for copy in copies:
        copy.start()

    for span in border:
        correlate(last % 3, span)
        base(last, 1, span, spread(last % 3, 1, span))

    def complete(turn, field):
        rows = rows_of(turn)

        def act(side):
            last_copy(turn, field, 1 - side).wait_recv()
            layers = added(last - 2, field, side, ghost[side], rows)
            more = [speed[border[side].start + cell, rows] * terms(side, cell, layers) for cell in range(REACH)]
            put(then, field, border[side], rows, more)

        on_sides(act)

    for turn in range(chunks):
        for field in range(2):
            complete(turn, field)
        rows = rows_of(turn)
        chunk = lax.rem(shot * slab // tall + 1 + turn, chunks)
        for side in range(2):
            span = border[side]
            value = total[within(span), rows] + ext[then, 0, span, rows] * ext[then, 1, span, rows]
            for index in range(owners):
                edges[chunk * owners + index, side * REACH : (side + 1) * REACH] = value[
                    :, index * slab : (index + 1) * slab
                ]
        for index in range(owners):
            peer = chunk * owners + index

            @pl.when(peer != shot)
            def _():
                part_copy(1, edges, edges_arrived, lax.rem(peer - shot + shots, shots)).start()

    edge_copies = [part_copy(1, edges, edges_arrived, ahead) for ahead in range(1, shots)]

    def close(side):
        next_speed(side).wait_send()
        for field in range(2):
            for turn in range(chunks):
                last_copy(turn, field, side).wait_send()

    on_sides(close)
    summed = middle[shot]
    for copy, ahead in zip(copies, range(1, shots)):
        copy.wait()
        summed = summed + middle_arrived[ahead - 1]
    image[within(inner)] = summed / STEPS
    summed = edges[shot]
    for copy, ahead in zip(edge_copies, range(1, shots)):
        copy.wait()
        summed = summed + edges_arrived[ahead - 1]
    for side in range(2):
        image[within(border[side])] = summed[side * REACH : (side + 1) * REACH] / STEPS


def keep(ext, image, fields_out, image_out, store_sem):
    cells_x = fields_out.shape[2]
    stores = [pltpu.make_async_copy(image, image_out, store_sem.at[0])] + [
        pltpu.make_async_copy(ext.at[(STEPS - 1 + time) % 3, :, REACH : REACH + cells_x], fields_out.at[time], store_sem.at[1 + time])
        for time in range(2)
    ]
    for store in stores:
        store.start()
    for store in stores:
        store.wait()


def shards(wavefields, velocity, aperture):
    fields = wavefields[0]
    cells_x, rows_y, rows_z = fields.shape[2:]
    wide = cells_x + 2 * REACH
    shots = lax.axis_size("shot")
    slab = velocity.shape[1]
    chunks = max(rows_y // max(8, slab), 1)
    across = np.kron(band(wide), np.eye(rows_y, dtype=np.float32)) + np.kron(
        np.eye(wide, dtype=np.float32), band(rows_y)
    )
    left = np.concatenate([across, across], axis=1).astype(jnp.bfloat16)
    right = np.concatenate([band(rows_z)] * 2, axis=0).astype(jnp.bfloat16)
    grid = (wide, rows_y, rows_z)
    vmem = pl.BlockSpec(memory_space=pltpu.VMEM)
    anywhere = pl.BlockSpec(memory_space=pl.ANY)
    ext, image = pl.pallas_call(
        kernel,
        out_shape=(pltpu.VMEM((3, 2) + grid, jnp.float32), pltpu.VMEM(velocity.shape, jnp.float32)),
        in_specs=[anywhere] * 5,
        out_specs=(vmem, vmem),
        scratch_shapes=[
            pltpu.SMEM(aperture.shape, jnp.int32),
            pltpu.VMEM(left.shape, jnp.bfloat16),
            pltpu.VMEM(right.shape, jnp.bfloat16),
            pltpu.VMEM((STEPS - 1, 2, 2, REACH, rows_y, rows_z), jnp.float32),
            pltpu.VMEM((shots, wide, slab, rows_z), jnp.float32),
            pltpu.VMEM(grid, jnp.float32),
            pltpu.VMEM(grid, jnp.float32),
            pltpu.VMEM(grid, jnp.float32),
            pltpu.VMEM((2,) + grid, jnp.float32),
            pltpu.VMEM((cells_x, rows_y, rows_z), jnp.float32),
            pltpu.VMEM((shots, cells_x - 2 * REACH, slab, rows_z), jnp.float32),
            pltpu.VMEM((shots - 1, cells_x - 2 * REACH, slab, rows_z), jnp.float32),
            pltpu.VMEM((shots, 2 * REACH, slab, rows_z), jnp.float32),
            pltpu.VMEM((shots - 1, 2 * REACH, slab, rows_z), jnp.float32),
            pltpu.SemaphoreType.DMA((STEPS - 1 + chunks, 2, 2)),
            pltpu.SemaphoreType.DMA((STEPS - 1 + chunks, 2, 2)),
            pltpu.SemaphoreType.DMA((6, max(shots - 1, 2))),
            pltpu.SemaphoreType.DMA((6, max(shots - 1, 2))),
            pltpu.SemaphoreType.DMA((2, shots - 1)),
            pltpu.SemaphoreType.DMA((2, shots - 1)),
            pltpu.SemaphoreType.DMA((6,)),
        ],
        compiler_params=pltpu.CompilerParams(collective_id=0, has_side_effects=True),
    )(jnp.asarray(left), jnp.asarray(right), fields, velocity, aperture)
    finals, image = pl.pallas_call(
        keep,
        out_shape=(
            jax.ShapeDtypeStruct(fields.shape, jnp.float32),
            jax.ShapeDtypeStruct(velocity.shape, jnp.float32),
        ),
        in_specs=[vmem, vmem],
        out_specs=(anywhere, anywhere),
        scratch_shapes=[pltpu.SemaphoreType.DMA((3,))],
    )(
        pltpu.with_memory_space_constraint(ext, pltpu.VMEM),
        pltpu.with_memory_space_constraint(image, pltpu.VMEM),
    )
    return finals[None], image


def solution(mesh):
    in_specs = (
        P(("groups", "shot"), None, None, "space", None, None),
        P(("groups", "space"), "shot", None),
        P(("groups", "shot"), None),
    )
    out_specs = (
        P(("groups", "shot"), None, None, "space", None, None),
        P(("groups", "space"), "shot", None),
    )
    return jax.shard_map(shards, mesh=mesh, in_specs=in_specs, out_specs=out_specs, check_vma=False)
```

```python
import functools

import jax
import jax.numpy as jnp
import numpy as np
from jax import lax
from jax.experimental import pallas as pl
from jax.experimental.pallas import tpu as pltpu
from jax.sharding import PartitionSpec as P

STEPS = 8
REACH = 4


SCALE = 5040.0
CENTRE = -3.0 * 14350.0
WEIGHTS = (0.0, 8064.0, -1008.0, 128.0, -9.0)
MESH = pl.DeviceIdType.MESH


def band(size):
    matrix = np.zeros((size, size), np.float32)
    for reach in range(1, REACH + 1):
        matrix += np.float32(WEIGHTS[reach]) * (
            np.eye(size, k=reach, dtype=np.float32) + np.eye(size, k=-reach, dtype=np.float32)
        )
    return matrix


def kernel(
    left, right, waves, velocity, aperture, ext, image,
    bounds, left_ref, right_ref, outer, speeds, speed, gain, inside, lap, total,
    middle, middle_arrived, edges, edges_arrived,
    halo_send, halo_recv, speed_send, speed_recv, part_send, part_recv, local_sem,
):
    space = lax.axis_index("space")
    spaces = lax.axis_size("space")
    shot = lax.axis_index("shot")
    shots = lax.axis_size("shot")
    wide, rows_y, rows_z = ext.shape[2:]
    cells_x, slab = velocity.shape[:2]
    flat = (wide * rows_y, rows_z)
    own = slice(REACH, REACH + cells_x)
    ghost = (slice(0, REACH), slice(wide - REACH, wide))
    border = (slice(REACH, 2 * REACH), slice(wide - 2 * REACH, wide - REACH))
    beyond = (slice(2 * REACH, 3 * REACH), slice(wide - 3 * REACH, wide - 2 * REACH))
    inner = slice(2 * REACH, wide - 2 * REACH)
    last = STEPS - 1
    chunks = halo_send.shape[0] - STEPS + 1
    tall = rows_y // chunks
    owners = shots // chunks
    has = (space > 0, space < spaces - 1)
    beside = (space - 1, space + 1)

    def within(span):
        return slice(span.start - REACH, span.stop - REACH)

    loads = [
        pltpu.make_async_copy(source, target, local_sem.at[at])
        for at, (source, target) in enumerate(
            (
                (waves.at[1], ext.at[0, :, own]),
                (velocity, speeds.at[shot, own]),
                (aperture, bounds),
                (left, left_ref),
                (right, right_ref),
                (waves.at[0], ext.at[2, :, own]),
            )
        )
    ]
    barrier = pltpu.get_barrier_semaphore()
    for side in range(2):
        @pl.when(has[side])
        def _():
            pl.semaphore_signal(barrier, inc=1, device_id={"space": beside[side]}, device_id_type=MESH)

    for ahead in range(1, shots):
        peer = lax.rem(shot + ahead, shots)
        pl.semaphore_signal(barrier, inc=1, device_id={"shot": peer}, device_id_type=MESH)
    for load in loads:
        load.start()

    pl.semaphore_wait(barrier, shots - 1 + jnp.where(has[0], 1, 0) + jnp.where(has[1], 1, 0))

    loads[0].wait()

    def message(source, target, slot, field, side):
        return pltpu.make_async_remote_copy(
            source,
            target,
            halo_send.at[slot, field, side],
            halo_recv.at[slot, field, 1 - side],
            device_id={"space": beside[side]},
            device_id_type=MESH,
        )

    def first_copy(field, side):
        return message(ext.at[0, field, border[side]], outer.at[STEPS - 2, field, 1 - side], 0, field, side)

    def second_copy(field, side):
        return message(ext.at[1, field, border[side]], ext.at[1, field, ghost[1 - side]], 1, field, side)

    def outer_copy(index, field, side):
        return message(
            ext.at[lax.rem(index, 3), field, beyond[side]],
            outer.at[index - 1, field, 1 - side],
            index + 1,
            field,
            side,
        )

    def rows_of(turn):
        chunk = lax.rem(shot * slab // tall + 1 + turn, chunks)
        return pl.ds(pl.multiple_of(chunk * tall, tall), tall)

    def last_copy(turn, field, side):
        rows = rows_of(turn)
        return message(
            ext.at[(last - 1) % 3, field, beyond[side], rows],
            outer.at[last - 2, field, 1 - side, :, rows],
            STEPS - 1 + turn,
            field,
            side,
        )

    def on_sides(act):
        for side in range(2):
            @pl.when(has[side])
            def _():
                act(side)

    def speed_copy(kind, side_or_span, ahead):
        return pltpu.make_async_remote_copy(
            speeds.at[shot, side_or_span],
            speeds.at[shot, side_or_span],
            speed_send.at[kind, ahead - 1],
            speed_recv.at[kind, ahead - 1],
            device_id={"shot": lax.rem(shot + ahead, shots)},
            device_id_type=MESH,
        )

    def next_speed(side):
        return pltpu.make_async_remote_copy(
            speeds.at[shot, border[side]],
            speeds.at[shot, ghost[1 - side]],
            speed_send.at[5, side],
            speed_recv.at[5, 1 - side],
            device_id={"space": beside[side]},
            device_id_type=MESH,
        )

    def ghost_speed(side, ahead):
        return pltpu.make_async_remote_copy(
            speeds.at[shot, ghost[side]],
            speeds.at[shot, ghost[side]],
            speed_send.at[3 + side, ahead - 1],
            speed_recv.at[3 + side, ahead - 1],
            device_id={"shot": lax.rem(shot + ahead, shots)},
            device_id_type=MESH,
        )

    spans = border + (inner,)
    on_sides(lambda side: first_copy(0, side).start())
    loads[1].wait()
    for kind in range(2):
        for ahead in range(1, shots):
            speed_copy(kind, spans[kind], ahead).start()
    on_sides(lambda side: first_copy(1, side).start())
    on_sides(lambda side: next_speed(side).start())
    for ahead in range(1, shots):
        speed_copy(2, spans[2], ahead).start()

    global_x = space * cells_x - REACH + lax.broadcasted_iota(jnp.int32, inside.shape, 0)
    loads[2].wait()
    seen = (global_x >= bounds[0, 0]) & (global_x < bounds[0, 1])
    inside[...] = jnp.where(seen, 1.0, 0.0)

    none = jnp.zeros((REACH, rows_y, rows_z), jnp.float32)
    for side in range(2):
        for field in range(2):
            ext[0, field, ghost[side]] = none

        @pl.when(jnp.logical_not(has[side]))
        def _():
            speed[ghost[side]] = none
            gain[ghost[side]] = none
            for field in range(2):
                ext[1, field, ghost[side]] = none

    def weigh(span):
        for index in range(shots):
            speed[span, index * slab : (index + 1) * slab, :] = speeds[index, span]
        scaled = speed[span] * inside[span] * (1.0 / SCALE)
        speed[span] = scaled
        gain[span] = 2.0 * inside[span] + CENTRE * scaled

    def gather(kind):
        for ahead in range(1, shots):
            speed_copy(kind, spans[kind], ahead).wait()
        weigh(spans[kind])

    def gather_ghost(side):
        for ahead in range(1, shots):
            ghost_speed(side, ahead).wait()
        weigh(ghost[side])

    def spread(now, field, span):
        cells = ext[now, field].reshape(flat)
        high = cells.astype(jnp.bfloat16)
        low = (cells - high.astype(jnp.float32)).astype(jnp.bfloat16)
        rows = slice(span.start * rows_y, span.stop * rows_y)
        return (
            jnp.dot(left_ref[rows], jnp.concatenate([high, low], axis=0), preferred_element_type=jnp.float32)
            + jnp.dot(
                jnp.concatenate([high[rows], low[rows]], axis=1), right_ref[...], preferred_element_type=jnp.float32
            )
        ).reshape((span.stop - span.start, rows_y, rows_z))

    def base(index, field, cells, around, masked=False):
        now, then, earlier = (lax.rem(index + ahead, 3) for ahead in range(3))
        before = ext[earlier, field, cells]
        if masked:
            before = inside[cells] * before
        ext[then, field, cells] = gain[cells] * ext[now, field, cells] - before + speed[cells] * around

    def correlate(then, cells):
        at = within(cells)
        total[at] = total[at] + ext[then, 0, cells] * ext[then, 1, cells]

    def terms(side, cell, layers):
        if side == 0:
            parts = [WEIGHTS[cell + REACH - layer] * layers[layer] for layer in range(cell, REACH)]
        else:
            parts = [WEIGHTS[REACH + layer - cell] * layers[layer] for layer in range(cell + 1)]
        return sum(parts[1:], parts[0])

    def added(slot, field, side, target, rows):
        layers = [outer[slot, field, side, layer, rows] for layer in range(REACH)]
        return [speed[target.start + cell, rows] * terms(side, cell, layers) for cell in range(REACH)]

    def put(then, field, target, rows, more):
        for cell in range(REACH):
            at = target.start + cell
            ext[then, field, at, rows] = ext[then, field, at, rows] + more[cell]

    every = slice(0, rows_y)

    def arrive(index, then, field):
        def act(side):
            outer_copy(index, field, 1 - side).wait_recv()
            put(then, field, ghost[side], every, added(index - 1, field, side, ghost[side], every))
        on_sides(act)

    for at in range(3, 5):
        loads[at].wait()

    def hand_on(side):
        next_speed(1 - side).wait_recv()
        for ahead in range(1, shots):
            ghost_speed(side, ahead).start()

    for field in range(2):
        lap[field, own] = spread(0, field, own)
    loads[5].wait()
    for kind in range(2):
        gather(kind)
        for field in range(2):
            base(0, field, border[kind], lap[field, border[kind]], True)

    def second(field):
        def act(side):
            first_copy(field, 1 - side).wait_recv()
            put(1, field, border[side], every, added(STEPS - 2, field, side, border[side], every))
            second_copy(field, side).start()
        on_sides(act)

    for field in range(2):
        second(field)
    on_sides(hand_on)
    gather(2)
    for field in range(2):
        base(0, field, inner, lap[field, inner], True)
        on_sides(lambda side: outer_copy(1, field, side).start())

    def settle(side):
        for field in range(2):
            ext[0, field, ghost[side]] = outer[STEPS - 2, field, side]

    on_sides(settle)
    total[...] = ext[1, 0, own] * ext[1, 1, own]
    on_sides(gather_ghost)

    everything = slice(0, wide)
    for field in range(2):
        on_sides(lambda side: second_copy(field, 1 - side).wait_recv())
        base(1, field, everything, spread(1, field, everything), True)
        on_sides(lambda side: outer_copy(2, field, side).start())
    correlate(2, own)
    for field in range(2):
        on_sides(lambda side: first_copy(field, side).wait_send())
        on_sides(lambda side: second_copy(field, side).wait_send())

    def step(index, carry):
        now = lax.rem(index, 3)
        for field in range(2):
            arrive(index - 1, now, field)

            @pl.when(index > 2)
            def _():
                on_sides(lambda side: outer_copy(index - 2, field, side).wait_send())

            base(index, field, everything, spread(now, field, everything))

            @pl.when(index < last - 2)
            def _():
                on_sides(lambda side: outer_copy(index + 1, field, side).start())

            @pl.when(index == last - 2)
            def _():
                if field == 0:
                    on_sides(lambda side: last_copy(0, 0, side).start())
                else:
                    on_sides(lambda side: last_copy(0, 1, side).start())
                    for turn in range(1, chunks):
                        for late in range(2):
                            on_sides(lambda side: last_copy(turn, late, side).start())

        correlate(lax.rem(index + 1, 3), own)
        return carry

    lax.fori_loop(2, last - 1, step, 0)

    then = STEPS % 3

    def part_copy(kind, source, target, ahead):
        peer = lax.rem(shot + ahead, shots)
        return pltpu.make_async_remote_copy(
            source.at[peer],
            target.at[ahead - 1],
            part_send.at[kind, ahead - 1],
            part_recv.at[kind, ahead - 1],
            device_id={"shot": peer},
            device_id_type=MESH,
        )

    for field in range(2):
        arrive(last - 2, (last - 1) % 3, field)
        on_sides(lambda side: outer_copy(last - 3, field, side).wait_send())
        base(last - 1, field, everything, spread((last - 1) % 3, field, everything))
        on_sides(lambda side: outer_copy(last - 2, field, side).wait_send())
        for span in (inner,) + border * (1 - field):
            base(last, field, span, spread(last % 3, field, span))
    correlate(last % 3, inner)
    correlate(then, inner)
    for index in range(shots):
        middle[index] = total[within(inner), index * slab : (index + 1) * slab, :]
    copies = [part_copy(0, middle, middle_arrived, ahead) for ahead in range(1, shots)]
    for copy in copies[1:] + copies[:1]:
        copy.start()

    for span in border:
        correlate(last % 3, span)
        base(last, 1, span, spread(last % 3, 1, span))

    def complete(turn, field):
        rows = rows_of(turn)

        def act(side):
            last_copy(turn, field, 1 - side).wait_recv()
            layers = added(last - 2, field, side, ghost[side], rows)
            more = [speed[border[side].start + cell, rows] * terms(side, cell, layers) for cell in range(REACH)]
            put(then, field, border[side], rows, more)

        on_sides(act)

    for turn in range(chunks):
        for field in range(2):
            complete(turn, field)
        rows = rows_of(turn)
        chunk = lax.rem(shot * slab // tall + 1 + turn, chunks)
        for side in range(2):
            span = border[side]
            value = total[within(span), rows] + ext[then, 0, span, rows] * ext[then, 1, span, rows]
            for index in range(owners):
                edges[chunk * owners + index, side * REACH : (side + 1) * REACH] = value[
                    :, index * slab : (index + 1) * slab
                ]
        for index in range(owners):
            peer = chunk * owners + index

            @pl.when(peer != shot)
            def _():
                part_copy(1, edges, edges_arrived, lax.rem(peer - shot + shots, shots)).start()

    edge_copies = [part_copy(1, edges, edges_arrived, ahead) for ahead in range(1, shots)]

    def close(side):
        next_speed(side).wait_send()
        for field in range(2):
            for turn in range(chunks):
                last_copy(turn, field, side).wait_send()

    on_sides(close)
    summed = middle[shot]
    for copy, ahead in zip(copies, range(1, shots)):
        copy.wait()
        summed = summed + middle_arrived[ahead - 1]
    image[within(inner)] = summed / STEPS
    summed = edges[shot]
    for copy, ahead in zip(edge_copies, range(1, shots)):
        copy.wait()
        summed = summed + edges_arrived[ahead - 1]
    for side in range(2):
        image[within(border[side])] = summed[side * REACH : (side + 1) * REACH] / STEPS


def keep(ext, image, fields_out, image_out, store_sem):
    cells_x = fields_out.shape[2]
    stores = [pltpu.make_async_copy(image, image_out, store_sem.at[0])] + [
        pltpu.make_async_copy(ext.at[(STEPS - 1 + time) % 3, :, REACH : REACH + cells_x], fields_out.at[time], store_sem.at[1 + time])
        for time in range(2)
    ]
    for store in stores[::-1]:
        store.start()
    for store in stores:
        store.wait()


def shards(wavefields, velocity, aperture):
    fields = wavefields[0]
    cells_x, rows_y, rows_z = fields.shape[2:]
    wide = cells_x + 2 * REACH
    shots = lax.axis_size("shot")
    slab = velocity.shape[1]
    chunks = max(rows_y // max(8, slab), 1)
    across = np.kron(band(wide), np.eye(rows_y, dtype=np.float32)) + np.kron(
        np.eye(wide, dtype=np.float32), band(rows_y)
    )
    left = np.concatenate([across, across], axis=1).astype(jnp.bfloat16)
    right = np.concatenate([band(rows_z)] * 2, axis=0).astype(jnp.bfloat16)
    grid = (wide, rows_y, rows_z)
    vmem = pl.BlockSpec(memory_space=pltpu.VMEM)
    anywhere = pl.BlockSpec(memory_space=pl.ANY)
    ext, image = pl.pallas_call(
        kernel,
        out_shape=(pltpu.VMEM((3, 2) + grid, jnp.float32), pltpu.VMEM(velocity.shape, jnp.float32)),
        in_specs=[anywhere] * 5,
        out_specs=(vmem, vmem),
        scratch_shapes=[
            pltpu.SMEM(aperture.shape, jnp.int32),
            pltpu.VMEM(left.shape, jnp.bfloat16),
            pltpu.VMEM(right.shape, jnp.bfloat16),
            pltpu.VMEM((STEPS - 1, 2, 2, REACH, rows_y, rows_z), jnp.float32),
            pltpu.VMEM((shots, wide, slab, rows_z), jnp.float32),
            pltpu.VMEM(grid, jnp.float32),
            pltpu.VMEM(grid, jnp.float32),
            pltpu.VMEM(grid, jnp.float32),
            pltpu.VMEM((2,) + grid, jnp.float32),
            pltpu.VMEM((cells_x, rows_y, rows_z), jnp.float32),
            pltpu.VMEM((shots, cells_x - 2 * REACH, slab, rows_z), jnp.float32),
            pltpu.VMEM((shots - 1, cells_x - 2 * REACH, slab, rows_z), jnp.float32),
            pltpu.VMEM((shots, 2 * REACH, slab, rows_z), jnp.float32),
            pltpu.VMEM((shots - 1, 2 * REACH, slab, rows_z), jnp.float32),
            pltpu.SemaphoreType.DMA((STEPS - 1 + chunks, 2, 2)),
            pltpu.SemaphoreType.DMA((STEPS - 1 + chunks, 2, 2)),
            pltpu.SemaphoreType.DMA((6, max(shots - 1, 2))),
            pltpu.SemaphoreType.DMA((6, max(shots - 1, 2))),
            pltpu.SemaphoreType.DMA((2, shots - 1)),
            pltpu.SemaphoreType.DMA((2, shots - 1)),
            pltpu.SemaphoreType.DMA((6,)),
        ],
        compiler_params=pltpu.CompilerParams(collective_id=0, has_side_effects=True),
    )(jnp.asarray(left), jnp.asarray(right), fields, velocity, aperture)
    finals, image = pl.pallas_call(
        keep,
        out_shape=(
            jax.ShapeDtypeStruct(fields.shape, jnp.float32),
            jax.ShapeDtypeStruct(velocity.shape, jnp.float32),
        ),
        in_specs=[vmem, vmem],
        out_specs=(anywhere, anywhere),
        scratch_shapes=[pltpu.SemaphoreType.DMA((3,))],
    )(
        pltpu.with_memory_space_constraint(ext, pltpu.VMEM),
        pltpu.with_memory_space_constraint(image, pltpu.VMEM),
    )
    return finals[None], image


def solution(mesh):
    in_specs = (
        P(("groups", "shot"), None, None, "space", None, None),
        P(("groups", "space"), "shot", None),
        P(("groups", "shot"), None),
    )
    out_specs = (
        P(("groups", "shot"), None, None, "space", None, None),
        P(("groups", "space"), "shot", None),
    )
    return jax.shard_map(shards, mesh=mesh, in_specs=in_specs, out_specs=out_specs, check_vma=False)
```
